32 devices in a mesh: groups: 2 (over y), dp: 4 (over x, core), ctx: 4 (over z).
Axes of the slice: x: 2, y: 2, z: 4, core: 2. Of those that a mesh axis runs over, the one named last changes fastest.
Arguments:
- normed_input: bfloat16 [8, 1024, 4096], P(('groups', 'dp'), 'ctx'), parts along dimension 0, may hold values from -6 to 6
- query_weight: bfloat16 [4096, 1024], P(('dp', 'ctx')), may hold values from -0.09375 to 0.09375
- key_vectors: bfloat16 [8, 1024, 1024], P(('groups', 'dp'), 'ctx'), parts along dimension 0, may hold values from -6 to 6
- value_vectors: bfloat16 [8, 1024, 1024], P(('groups', 'dp'), 'ctx'), parts along dimension 0, may hold values from -6 to 6
- input_gate: float32 [8, 4, 1024], P(('groups', 'dp'), None, 'ctx'), parts along dimension 0, may hold values from -16 to 210
- forget_gate: float32 [8, 4, 1024], P(('groups', 'dp'), None, 'ctx'), parts along dimension 0
- resets: int32 [8, 1024], P(('groups', 'dp'), 'ctx'), parts along dimension 0, may hold values 0 or 1
Outputs:
- hidden: bfloat16 [8, 1024, 1024], P(('groups', 'dp'), 'ctx'), parts along dimension 0
The draws below stay inside these ranges and needn't reach their ends.
There are 2 independent parts, one for each index of `groups`. The reference program is written for one: setup_inputs(seed, part) draws one part's arguments, and reference() takes and returns one part's arrays. A program takes and returns all parts, laid end to end along the dimension named above; an argument that names none is the same for every part. Nothing has to cross between parts.
Inputs may be any that keep to these rules, and one draw needn't show every extreme that they name: `resets`: 1 where a new document begins at that position.
All inputs are finite; a program needn't handle non-finite values. No bound on the sum of `resets` on one device may be relied on, other than what follows from the above.
Results may differ from the reference program's by a relative error of at most 0.009.
Values may be sent and summed in bfloat16 or wider, within the bound.
No kernel may reach another device: no remote copies, remote signals or barrier semaphores. Data moves between devices by JAX's collectives and lax.ppermute only.
A program may use at most 128 MiB of HBM per device.

```python
import math
import jax
import jax.numpy as jnp
from jax import lax

D = 4096
LOCAL_HEADS = 4
DQK = 256
DV = 256
TOK_DEV = 256
SEQUENCE_LENGTH = 1024
GROUP_SEQUENCES = 4


def head_ranking(one_key):
    return jax.random.permutation(one_key, LOCAL_HEADS)


def draw_forget_gate(key, part):
    random_subkeys = jax.random.split(jax.random.fold_in(key, 11), 7)
    ranking = jax.vmap(head_ranking)(jax.random.split(random_subkeys[0], GROUP_SEQUENCES))
    slow_head = ranking < LOCAL_HEADS // 2
    head_shape = (GROUP_SEQUENCES, LOCAL_HEADS, 1, 1)
    slow_rate = jnp.exp(jax.random.uniform(random_subkeys[1], head_shape, minval=math.log(0.2), maxval=math.log(0.8))) / SEQUENCE_LENGTH
    fast_rate = jnp.exp(jax.random.uniform(random_subkeys[2], head_shape, minval=math.log(1.0 / 50.0), maxval=math.log(1.0 / 30.0)))
    base_rate = jnp.where(slow_head[:, :, None, None], slow_rate, fast_rate)
    block_count = SEQUENCE_LENGTH // TOK_DEV
    device_factor = jnp.exp(jax.random.uniform(random_subkeys[3], (GROUP_SEQUENCES, LOCAL_HEADS, block_count, 1), minval=math.log(0.5), maxval=math.log(2.0)))
    token_factor = jnp.exp(jax.random.uniform(random_subkeys[4], (GROUP_SEQUENCES, LOCAL_HEADS, block_count, TOK_DEV), minval=math.log(0.5), maxval=math.log(2.0)))
    decay_rate = (base_rate * device_factor * token_factor).reshape(GROUP_SEQUENCES, LOCAL_HEADS, SEQUENCE_LENGTH)
    stable_mask = -decay_rate - jnp.log(-jnp.expm1(-decay_rate))
    sudden_mask = jax.random.bernoulli(random_subkeys[5], 2.0 / SEQUENCE_LENGTH, (GROUP_SEQUENCES, 1, SEQUENCE_LENGTH))
    sudden_keep = jax.random.uniform(random_subkeys[6], (GROUP_SEQUENCES, LOCAL_HEADS, SEQUENCE_LENGTH), minval=0.5, maxval=0.8)
    return jnp.where(sudden_mask, jnp.log(sudden_keep / (1.0 - sudden_keep)), stable_mask)


def draw_input_gate(key, part):
    random_subkeys = jax.random.split(jax.random.fold_in(key, 23), 1)
    gate_shape = (GROUP_SEQUENCES, LOCAL_HEADS, SEQUENCE_LENGTH)
    return jnp.clip(-8.0 + 2.5 * jax.random.normal(random_subkeys[0], gate_shape), -16.0, 0.0)


def touch_ends(values, own_key, smallest, top_value):
    extent = values.shape
    index_at = [jax.random.randint(jax.random.fold_in(own_key, axis), (), 0, extent[axis]) for axis in range(len(extent))]
    values = values.at[tuple(index_at)].set(smallest)
    longest = extent.index(max(extent))
    index_at[longest] = (index_at[longest] + 1) % extent[longest]
    return values.at[tuple(index_at)].set(top_value)


def steps_of(rng, dims, shards, least, high):
    def one(axis_at, parts):
        draws = jax.random.uniform(jax.random.fold_in(jax.random.fold_in(rng, 6), axis_at), (parts,), jnp.float32, least / len(shards), high / len(shards))
        return jnp.repeat(jnp.exp(draws), dims[axis_at] // parts).reshape((-1,) + (1,) * (len(dims) - axis_at - 1))

    level = one(*shards[0])
    for cut in shards[1:]:
        level = level * one(*cut)
    return level


def centred(own_key, shape, deviation, reach, cuts=(), kind=jnp.bfloat16):
    result = jax.random.normal(own_key, shape, jnp.float32) * deviation
    if len(cuts) > 0:
        result = steps_of(own_key, shape, cuts, -0.22, 0.18) * result
    return jnp.clip(result, min=-reach, max=reach).astype(kind)


def setup_inputs(seed: int = 0, part: int = 0) -> dict:
    keys = jax.random.split(jax.random.key(seed), 8)
    part_splits = jax.random.split(jax.random.fold_in(keys[7], part), 8)
    return {
        "normed_input": centred(part_splits[0], (GROUP_SEQUENCES, SEQUENCE_LENGTH, D), 1.0, 6.0, ((0, 4), (1, 4))),
        "query_weight": centred(keys[1], (D, LOCAL_HEADS * DQK), D ** -0.5, 0.09375, ((0, 16),)),
        "key_vectors": centred(part_splits[2], (GROUP_SEQUENCES, SEQUENCE_LENGTH, LOCAL_HEADS * DQK), 1.0, 6.0, ((0, 4), (1, 4))),
        "value_vectors": centred(part_splits[3], (GROUP_SEQUENCES, SEQUENCE_LENGTH, LOCAL_HEADS * DV), 1.0, 6.0, ((0, 4), (1, 4))),
        "input_gate": draw_input_gate(jax.random.fold_in(jax.random.fold_in(keys[7], part), 71), part),
        "forget_gate": draw_forget_gate(jax.random.fold_in(jax.random.fold_in(keys[7], part), 71), part),
        "resets": touch_ends((jax.random.randint(part_splits[6], (GROUP_SEQUENCES, SEQUENCE_LENGTH), 0, SEQUENCE_LENGTH) < 1).astype(jnp.int32), jax.random.fold_in(part_splits[6], 1), 0, 1),
    }


very_low = -1.0e30


def wide_einsum(form, left, right):
    return jnp.einsum(form, left.astype(jnp.float32), right.astype(jnp.float32), precision=lax.Precision.HIGHEST)


def block_step(state, block):
    matrix_memory, normer, log_max = state
    query_tile, key_block, value_tile, gate_block, forget_block, flag_block = block
    score_factor = DQK ** -0.5
    reset_count = jnp.cumsum(flag_block)
    cumulative = jnp.cumsum(forget_block, axis=1)
    positions = jnp.arange(flag_block.shape[0])
    linked = jnp.logical_and(reset_count[:, None] == reset_count[None, :], positions[:, None] >= positions[None, :])
    exponent = jnp.where(linked[None], cumulative[:, :, None] - cumulative[:, None, :] + gate_block[:, None, :], very_low)
    carried = jnp.where(reset_count[None, :] == 0, cumulative + log_max[:, None], very_low)
    row_max = jnp.maximum(jnp.max(exponent, axis=2), carried)
    scores = wide_einsum("thk,shk->hts", query_tile, key_block) * score_factor
    weighted_scores = (jnp.exp(exponent - row_max[:, :, None]) * scores).astype(jnp.bfloat16)
    carry_scale = jnp.exp(carried - row_max)
    cross_numerator = wide_einsum("ngu,gus->ngs", query_tile, matrix_memory.astype(jnp.bfloat16)) * score_factor
    inter_den = wide_einsum("thk,hk->th", query_tile, normer.astype(jnp.bfloat16)) * score_factor
    numerator = wide_einsum("hts,shv->thv", weighted_scores, value_tile)
    numerator = numerator + carry_scale.T[:, :, None] * cross_numerator
    denominator = jnp.sum(weighted_scores.astype(jnp.float32), axis=2).T + carry_scale.T * inter_den
    floor_value = jnp.exp(jnp.maximum(-row_max, 0.0)).T
    hidden = numerator / jnp.maximum(jnp.abs(denominator), floor_value)[:, :, None]
    chain_total = cumulative[:, -1]
    end_expo = jnp.where((reset_count == reset_count[-1])[None, :], chain_total[:, None] - cumulative + gate_block, very_low)
    keep_expo = jnp.where(reset_count[-1] == 0, chain_total + log_max, very_low)
    new_max = jnp.maximum(jnp.max(end_expo, axis=1), keep_expo)
    token_weight = jnp.exp(end_expo - new_max[:, None])
    retain_weight = jnp.exp(keep_expo - new_max)
    key_weighted = (key_block.astype(jnp.float32) * token_weight.T[:, :, None]).astype(jnp.bfloat16)
    matrix_memory = retain_weight[:, None, None] * matrix_memory + wide_einsum("oga,ogu->gau", key_weighted, value_tile)
    normer = retain_weight[:, None] * normer + jnp.sum(key_weighted.astype(jnp.float32), axis=0)
    return (matrix_memory, normer, new_max), hidden


def reference(normed_input, query_weight, key_vectors, value_vectors, input_gate, forget_gate, resets):
    projected = jnp.dot(normed_input.reshape(GROUP_SEQUENCES * SEQUENCE_LENGTH, D).astype(jnp.float32), query_weight.astype(jnp.float32), precision=lax.Precision.HIGHEST).astype(jnp.bfloat16)
    projected = projected.reshape(GROUP_SEQUENCES, SEQUENCE_LENGTH, LOCAL_HEADS, DQK)
    key_heads = key_vectors.reshape(GROUP_SEQUENCES, SEQUENCE_LENGTH, LOCAL_HEADS, DQK)
    value_heads = value_vectors.reshape(GROUP_SEQUENCES, SEQUENCE_LENGTH, LOCAL_HEADS, DV)
    log_forget = jax.nn.log_sigmoid(forget_gate)
    block_len = TOK_DEV
    block_count = SEQUENCE_LENGTH // block_len

    def one_sequence(sequence_item):
        query_seq, key_seq, value_seq, gate_seq, forget_seq, flag_seq = sequence_item
        blocks = (
            query_seq.reshape(block_count, block_len, LOCAL_HEADS, DQK),
            key_seq.reshape(block_count, block_len, LOCAL_HEADS, DQK),
            value_seq.reshape(block_count, block_len, LOCAL_HEADS, DV),
            gate_seq.reshape(LOCAL_HEADS, block_count, block_len).transpose(1, 0, 2),
            forget_seq.reshape(LOCAL_HEADS, block_count, block_len).transpose(1, 0, 2),
            flag_seq.reshape(block_count, block_len),
        )
        start_state = (
            jnp.zeros((LOCAL_HEADS, DQK, DV), jnp.float32),
            jnp.zeros((LOCAL_HEADS, DQK), jnp.float32),
            jnp.full((LOCAL_HEADS,), very_low, jnp.float32),
        )
        final_state, hidden = lax.scan(block_step, start_state, blocks)
        return hidden.reshape(SEQUENCE_LENGTH, LOCAL_HEADS * DV)

    hidden = lax.map(one_sequence, (projected, key_heads, value_heads, input_gate, log_forget, resets))
    return hidden.astype(jnp.bfloat16)
```

```python
import functools

import jax
import jax.numpy as jnp
from jax import lax
from jax.experimental import pallas as pl
from jax.experimental.pallas import tpu as pltpu
from jax.sharding import PartitionSpec as P


very_low = -1e30
AXES = ("groups", "dp", "ctx")
CORES = 2
EXTRA = 16
f32 = jnp.float32
bf16 = jnp.bfloat16


def moves(mesh, where):
    ng, nd, nz = (mesh.shape[a] for a in AXES)
    pairs = []
    for g in range(ng):
        for x in range(nd // CORES):
            for k in range(CORES):
                for z in range(nz):
                    to = where(g, x, k, z)
                    if to is not None:
                        g2, x2, k2, z2 = to
                        source = (g * nd + x * CORES + k) * nz + z
                        pairs.append((source, (g2 * nd + x2 * CORES + k2) * nz + z2))
    return pairs


def lane_scan(values):
    length = values.shape[1]
    lane = lax.broadcasted_iota(jnp.int32, values.shape, 1)
    step = 1
    while step < length:
        moved = pltpu.roll(values, step, 1)
        values = values + jnp.where(lane >= step, moved, jnp.zeros_like(values))
        step *= 2
    return values


def log_sigmoid(x):
    return jnp.minimum(x, 0.0) - jnp.log1p(jnp.exp(-jnp.abs(x)))


def padded(values):
    rows = values.shape[0]
    if rows % 8 == 0:
        return values
    fill = jnp.zeros((8 - rows % 8, values.shape[1]), values.dtype)
    return jnp.concatenate([values, fill], axis=0)


def split_rows(value):
    high = value.astype(bf16)
    rest = value - high.astype(f32)
    mid = rest.astype(bf16)
    low = (rest - mid.astype(f32)).astype(bf16)
    return high, mid, low


def store_message(out_ref, base, size, memory, normer, top):
    out_ref[base : base + size, :] = memory.astype(bf16)
    n_parts = split_rows(normer)
    t_parts = split_rows(jnp.broadcast_to(top, normer.shape))
    row = lax.broadcasted_iota(jnp.int32, (EXTRA, normer.shape[1]), 0)
    block = jnp.zeros((EXTRA, normer.shape[1]), f32)
    for i, part in enumerate(n_parts + t_parts):
        block = jnp.where(row == i, part.astype(f32), block)
    out_ref[base + size : base + size + EXTRA, :] = block.astype(bf16)


def load_message(ref, base, size):
    extra = ref[base + size : base + size + EXTRA, :].astype(f32)
    normer = extra[0:1] + extra[1:2] + extra[2:3]
    top = extra[3:4, 0:1] + extra[4:5, 0:1] + extra[5:6, 0:1]
    return ref[base : base + size, :], normer, top


def state_kernel(heads, k_ref, v_ref, gate_ref, forget_ref, reset_ref, own_ref, msg_ref, side_ref):
    size = k_ref.shape[1] // heads
    vsize = v_ref.shape[1] // heads
    length = k_ref.shape[0]
    count = lane_scan(padded(reset_ref[...].astype(f32)))[0:1]
    cumulative = lane_scan(padded(log_sigmoid(forget_ref[...])))[0:heads]
    total = cumulative[:, length - 1 : length]
    final = count[:, length - 1 : length]
    expo = jnp.where(count == final, total - cumulative + gate_ref[...], very_low)
    top = jnp.max(expo, axis=1, keepdims=True)
    weight = padded(jnp.exp(expo - top)).T
    gap = jnp.where(final > 0, very_low, total)
    stride = size + EXTRA
    for h in range(heads):
        keys = k_ref[:, h * size : (h + 1) * size].astype(f32)
        weighted = (keys * weight[:, h : h + 1]).astype(bf16)
        values = v_ref[:, h * vsize : (h + 1) * vsize]
        memory = lax.dot_general(
            weighted, values, (((0,), (0,)), ((), ())), preferred_element_type=f32
        )
        normer = jnp.sum(weighted.astype(f32), axis=0, keepdims=True)
        own_ref[h * size : (h + 1) * size, :] = memory
        side_ref[h * 8 : h * 8 + 1, :] = normer
        side_ref[h * 8 + 1 : h * 8 + 2, :] = jnp.broadcast_to(top[h : h + 1], normer.shape)
        side_ref[h * 8 + 2 : h * 8 + 3, :] = jnp.broadcast_to(gap[h : h + 1], normer.shape)
        store_message(msg_ref, h * stride, size, memory, normer, top[h : h + 1])


def combine_kernel(heads, prev_ref, own_ref, side_ref, msg_ref):
    size = own_ref.shape[0] // heads
    stride = size + EXTRA
    for h in range(heads):
        memory, normer, top = load_message(prev_ref, h * stride, size)
        own_normer = side_ref[h * 8 : h * 8 + 1, :]
        own_top = side_ref[h * 8 + 1 : h * 8 + 2, 0:1]
        gap = side_ref[h * 8 + 2 : h * 8 + 3, 0:1]
        shifted = top + gap
        both = jnp.maximum(shifted, own_top)
        early = jnp.exp(shifted - both)
        late = jnp.exp(own_top - both)
        joined = early * memory.astype(f32) + late * own_ref[h * size : (h + 1) * size, :]
        store_message(msg_ref, h * stride, size, joined, early * normer + late * own_normer, both)


def project_kernel(parts, nz, ng, x_ref, w_ref, *rest):
    pieces, (keep_ref, send_ref, whole) = rest[:parts], rest[parts:]
    rows = w_ref.shape[0]
    width = w_ref.shape[1] // ng
    nd = x_ref.shape[0]
    nx = nd // CORES
    group, dp, place = (lax.axis_index(a) for a in AXES)
    whole[pl.ds(pl.multiple_of(place * rows, rows), rows), :] = w_ref[...]
    at = 0
    for s in range(1, nz):
        row = pl.multiple_of((place ^ s) * rows, rows)
        for rel in range(ng):
            column = pl.multiple_of(lax.rem(group + rel, ng) * width, width)
            whole[pl.ds(row, rows), pl.ds(column, width)] = pieces[at][...]
            at += 1
    x, core = lax.div(dp, CORES), lax.rem(dp, CORES)
    for rel in range(nx):
        base = lax.rem(x + rel, nx) * CORES
        keep_ref[rel] = jnp.dot(x_ref[base + core], whole[...], preferred_element_type=f32)
        send_ref[rel] = jnp.dot(x_ref[base + 1 - core], whole[...], preferred_element_type=f32)


def read_kernel(
    heads, hops, arrivals, keep_ref, other_ref, *rest
):
    received = rest[:arrivals]
    k_ref, v_ref, gate_ref, forget_ref, reset_ref = rest[arrivals : arrivals + 5]
    states = rest[arrivals + 5 : arrivals + 5 + hops]
    out_ref, state, sem = rest[arrivals + 5 + hops :]
    size = k_ref.shape[1] // heads
    vsize = v_ref.shape[1] // heads
    length = k_ref.shape[0]
    factor = size ** (-0.5)
    stride = size + EXTRA
    place = lax.axis_index("ctx")
    for h in range(hops):

        @pl.when(place == h + 1)
        def _():
            copy = pltpu.make_async_copy(states[h], state, sem)
            copy.start()
            copy.wait()

    @pl.when(place == 0)
    def _():
        state[...] = jnp.zeros_like(state)

    count = lane_scan(padded(reset_ref[...].astype(f32)))
    cumulative = lane_scan(padded(log_sigmoid(forget_ref[...])))
    count_rows = count.T[:, 0:1]
    cumulative_rows = cumulative.T
    t_at = lax.broadcasted_iota(jnp.int32, (length, length), 0)
    s_at = lax.broadcasted_iota(jnp.int32, (length, length), 1)
    linked = jnp.logical_and(count_rows == count[0:1], t_at >= s_at)
    for h in range(heads):
        at = slice(h * size, (h + 1) * size)
        vat = slice(h * vsize, (h + 1) * vsize)
        total = keep_ref[:, at] + other_ref[:, at]
        for r in received:
            total = total + r[:, at].astype(f32)
        query = total.astype(bf16)
        keys, values = k_ref[:, at], v_ref[:, vat]
        memory, normer, top = load_message(state, h * stride, size)
        top = jnp.where(place == 0, very_low, top)
        cum_t = cumulative_rows[:, h : h + 1]
        exponent = jnp.where(
            linked, cum_t - cumulative[h : h + 1] + gate_ref[h : h + 1, :], very_low
        )
        carried = jnp.where(count_rows == 0.0, cum_t + top, very_low)
        row_max = jnp.maximum(jnp.max(exponent, axis=1, keepdims=True), carried)
        scores = lax.dot_general(
            query, keys, (((1,), (1,)), ((), ())), preferred_element_type=f32
        )
        weighted = (jnp.exp(exponent - row_max) * (scores * factor)).astype(bf16)
        scale = jnp.exp(carried - row_max) * factor
        cross = jnp.dot(query, memory, preferred_element_type=f32)
        normer = normer.astype(bf16).astype(f32)
        inter = jnp.sum(query.astype(f32) * normer, axis=1, keepdims=True)
        numerator = jnp.dot(weighted, values, preferred_element_type=f32) + scale * cross
        denominator = jnp.sum(weighted.astype(f32), axis=1, keepdims=True) + scale * inter
        floor = jnp.exp(jnp.maximum(-row_max, 0.0))
        out_ref[:, vat] = (numerator / jnp.maximum(jnp.abs(denominator), floor)).astype(bf16)


VMEM = pl.BlockSpec(memory_space=pltpu.VMEM)
ANY = pl.BlockSpec(memory_space=pl.ANY)


def make_body(mesh):
    ng, nd, nz = (mesh.shape[a] for a in AXES)
    nx = nd // CORES

    def send(value, where):
        return lax.ppermute(value, AXES, moves(mesh, where))

    def body(normed_input, query_weight, key_vectors, value_vectors, input_gate, forget_gate, resets):
        sequences, length, features = normed_input.shape
        heads = input_gate.shape[1]
        columns = query_weight.shape[1]
        width = columns // ng
        size = columns // heads
        keys, values = key_vectors[0], value_vectors[0]
        gate, forget = input_gate[0], forget_gate[0]
        vwidth = values.shape[1]
        group = lax.axis_index("groups")
        tokens = lax.all_to_all(normed_input, "dp", 2, 0, tiled=True)
        part = lax.dynamic_slice_in_dim(query_weight, group * width, width, 1)
        pieces = []
        for s in range(1, nz):
            mine = send(part, lambda g, x, k, z: (g, x, k, z ^ s))
            pieces.append(mine)
            for rel in range(1, ng):
                pieces.append(send(mine, lambda g, x, k, z: ((g - rel) % ng, x, k, z)))
        stride = size + EXTRA
        message = jax.ShapeDtypeStruct((heads * stride, vwidth // heads), bf16)
        own, first, side = pl.pallas_call(
            functools.partial(state_kernel, heads),
            out_shape=(
                jax.ShapeDtypeStruct((heads * size, vwidth // heads), f32),
                message,
                jax.ShapeDtypeStruct((heads * 8, vwidth // heads), f32),
            ),
            in_specs=[VMEM] * 5,
            out_specs=(VMEM,) * 3,
            name="own_state",
        )(keys, values, gate, forget, resets)
        states = []
        current = first
        for hop in range(1, nz):
            arrived = send(
                current, lambda g, x, k, z: (g, x, k, z + 1) if z == hop - 1 else None
            )
            states.append(arrived)
            if hop < nz - 1:
                current = pl.pallas_call(
                    functools.partial(combine_kernel, heads),
                    out_shape=message,
                    in_specs=[VMEM] * 3,
                    out_specs=VMEM,
                    name="combine",
                )(arrived, own, side)
        shape = jax.ShapeDtypeStruct((nx, length, columns), f32)
        keep, away = pl.pallas_call(
            functools.partial(project_kernel, len(pieces), nz, ng),
            out_shape=(shape, shape),
            in_specs=[VMEM] * (2 + len(pieces)),
            out_specs=(VMEM, VMEM),
            scratch_shapes=[pltpu.VMEM((query_weight.shape[0] * nz, columns), bf16)],
            name="project",
        )(tokens, query_weight, *pieces)
        other = send(away, lambda g, x, k, z: (g, x, 1 - k, z))
        received = []
        for rel in range(1, nx):
            total = (keep[rel] + other[rel]).astype(bf16)
            received.append(send(total, lambda g, x, k, z: (g, (x + rel) % nx, k, z)))
        hidden = pl.pallas_call(
            functools.partial(read_kernel, heads, len(states), len(received)),
            out_shape=jax.ShapeDtypeStruct((length, vwidth), bf16),
            in_specs=[VMEM] * (7 + len(received)) + [ANY] * len(states),
            out_specs=VMEM,
            scratch_shapes=[
                pltpu.VMEM(message.shape, bf16),
                pltpu.SemaphoreType.DMA(()),
            ],
            name="read_out",
        )(keep[0], other[0], *received, keys, values, gate, forget, resets, *states)
        return hidden[None]

    return body


def solution(mesh):
    return jax.shard_map(
        make_body(mesh),
        mesh=mesh,
        in_specs=(
            P(("groups", "dp"), "ctx", None),
            P(("dp", "ctx"), None),
            P(("groups", "dp"), "ctx", None),
            P(("groups", "dp"), "ctx", None),
            P(("groups", "dp"), None, "ctx"),
            P(("groups", "dp"), None, "ctx"),
            P(("groups", "dp"), "ctx"),
        ),
        out_specs=P(("groups", "dp"), "ctx", None),
        check_vma=False,
    )
```

```python
import functools

import jax
import jax.numpy as jnp
from jax import lax
from jax.experimental import pallas as pl
from jax.experimental.pallas import tpu as pltpu
from jax.sharding import PartitionSpec as P


very_low = -1e30
AXES = ("groups", "dp", "ctx")
CORES = 2
EXTRA = 16
f32 = jnp.float32
bf16 = jnp.bfloat16


def moves(mesh, where):
    ng, nd, nz = (mesh.shape[a] for a in AXES)
    pairs = []
    for g in range(ng):
        for x in range(nd // CORES):
            for k in range(CORES):
                for z in range(nz):
                    to = where(g, x, k, z)
                    if to is not None:
                        g2, x2, k2, z2 = to
                        source = (g * nd + x * CORES + k) * nz + z
                        pairs.append((source, (g2 * nd + x2 * CORES + k2) * nz + z2))
    return pairs


def lane_scan(values):
    length = values.shape[1]
    lane = lax.broadcasted_iota(jnp.int32, values.shape, 1)
    step = 1
    while step < length:
        moved = pltpu.roll(values, step, 1)
        values = values + jnp.where(lane >= step, moved, jnp.zeros_like(values))
        step *= 2
    return values


def log_sigmoid(x):
    return jnp.minimum(x, 0.0) - jnp.log1p(jnp.exp(-jnp.abs(x)))


def padded(values):
    rows = values.shape[0]
    if rows % 8 == 0:
        return values
    fill = jnp.zeros((8 - rows % 8, values.shape[1]), values.dtype)
    return jnp.concatenate([values, fill], axis=0)


def split_rows(value):
    high = value.astype(bf16)
    rest = value - high.astype(f32)
    mid = rest.astype(bf16)
    low = (rest - mid.astype(f32)).astype(bf16)
    return high, mid, low


def store_message(out_ref, base, size, memory, normer, top):
    out_ref[base : base + size, :] = memory.astype(bf16)
    n_parts = split_rows(normer)
    t_parts = split_rows(jnp.broadcast_to(top, normer.shape))
    row = lax.broadcasted_iota(jnp.int32, (EXTRA, normer.shape[1]), 0)
    block = jnp.zeros((EXTRA, normer.shape[1]), f32)
    for i, part in enumerate(n_parts + t_parts):
        block = jnp.where(row == i, part.astype(f32), block)
    out_ref[base + size : base + size + EXTRA, :] = block.astype(bf16)


def load_message(ref, base, size):
    extra = ref[base + size : base + size + EXTRA, :].astype(f32)
    normer = extra[0:1] + extra[1:2] + extra[2:3]
    top = extra[3:4, 0:1] + extra[4:5, 0:1] + extra[5:6, 0:1]
    return ref[base : base + size, :], normer, top


def state_kernel(heads, k_ref, v_ref, gate_ref, forget_ref, reset_ref, own_ref, msg_ref, side_ref):
    size = k_ref.shape[1] // heads
    vsize = v_ref.shape[1] // heads
    length = k_ref.shape[0]
    count = lane_scan(padded(reset_ref[...].astype(f32)))[0:1]
    cumulative = lane_scan(padded(log_sigmoid(forget_ref[...])))[0:heads]
    total = cumulative[:, length - 1 : length]
    final = count[:, length - 1 : length]
    expo = jnp.where(count == final, total - cumulative + gate_ref[...], very_low)
    top = jnp.max(expo, axis=1, keepdims=True)
    weight = padded(jnp.exp(expo - top)).T
    gap = jnp.where(final > 0, very_low, total)
    stride = size + EXTRA
    for h in range(heads):
        keys = k_ref[:, h * size : (h + 1) * size].astype(f32)
        weighted = (keys * weight[:, h : h + 1]).astype(bf16)
        values = v_ref[:, h * vsize : (h + 1) * vsize]
        memory = lax.dot_general(
            weighted, values, (((0,), (0,)), ((), ())), preferred_element_type=f32
        )
        normer = jnp.sum(weighted.astype(f32), axis=0, keepdims=True)
        own_ref[h * size : (h + 1) * size, :] = memory
        side_ref[h * 8 : h * 8 + 1, :] = normer
        side_ref[h * 8 + 1 : h * 8 + 2, :] = jnp.broadcast_to(top[h : h + 1], normer.shape)
        side_ref[h * 8 + 2 : h * 8 + 3, :] = jnp.broadcast_to(gap[h : h + 1], normer.shape)
        store_message(msg_ref, h * stride, size, memory, normer, top[h : h + 1])


def combine_kernel(heads, prev_ref, own_ref, side_ref, msg_ref):
    size = own_ref.shape[0] // heads
    stride = size + EXTRA
    for h in range(heads):
        memory, normer, top = load_message(prev_ref, h * stride, size)
        own_normer = side_ref[h * 8 : h * 8 + 1, :]
        own_top = side_ref[h * 8 + 1 : h * 8 + 2, 0:1]
        gap = side_ref[h * 8 + 2 : h * 8 + 3, 0:1]
        shifted = top + gap
        both = jnp.maximum(shifted, own_top)
        early = jnp.exp(shifted - both)
        late = jnp.exp(own_top - both)
        joined = early * memory.astype(f32) + late * own_ref[h * size : (h + 1) * size, :]
        store_message(msg_ref, h * stride, size, joined, early * normer + late * own_normer, both)


def project_kernel(nz, nx, *refs):
    count = CORES * nx
    blocks, parts = refs[:count], refs[count : count + nz]
    keep_ref, send_ref, tokens, whole, sems = refs[count + nz :]
    rows = parts[0].shape[1]
    place = lax.axis_index("ctx")
    core = lax.rem(lax.axis_index("dp"), CORES)
    copies = []
    for s in range(nz):
        source = place ^ s
        for j in range(CORES):
            owner = lax.rem(core + j, CORES)
            row = pl.multiple_of((owner * nz + source) * rows, rows)
            copies.append((parts[s].at[j], whole.at[pl.ds(row, rows)]))
    sequence = list(range(CORES, count)) + list(range(CORES))
    for i in sequence:
        copies.append((blocks[i], tokens.at[i]))
    started = []
    for i, (source, target) in enumerate(copies):
        copy = pltpu.make_async_copy(source, target, sems.at[i])
        copy.start()
        started.append(copy)
    for copy in started[: nz * CORES]:
        copy.wait()
    for at, i in enumerate(sequence):
        started[nz * CORES + at].wait()
        value = jnp.dot(tokens[i], whole[...], preferred_element_type=f32)
        if i >= CORES:
            send_ref[i // CORES - 1, i % CORES] = value.astype(bf16)
        else:
            keep_ref[i] = value


def read_kernel(
    heads, hops, phase, *rest
):
    mine_ref, theirs_ref, k_ref, v_ref, gate_ref, forget_ref, reset_ref = rest[:7]
    states = rest[7 : 7 + hops]
    earlier = rest[7 + hops] if phase else None
    out_ref, state, sem = rest[7 + hops + (1 if phase else 0) :]
    size = k_ref.shape[1] // heads
    vsize = v_ref.shape[1] // heads
    length = k_ref.shape[0]
    factor = size ** (-0.5)
    stride = size + EXTRA
    group, dp, place = (lax.axis_index(a) for a in AXES)
    core = lax.rem(dp, CORES)
    ng = heads // CORES
    for h in range(hops):

        @pl.when(place == h + 1)
        def _():
            copy = pltpu.make_async_copy(states[h], state, sem)
            copy.start()
            copy.wait()

    @pl.when(place == 0)
    def _():
        state[...] = jnp.zeros_like(state)

    def head_of(j, r):
        return lax.rem(core + j, CORES) * ng + lax.rem(group + r, ng)

    t_at = lax.broadcasted_iota(jnp.int32, (length, length), 0)
    s_at = lax.broadcasted_iota(jnp.int32, (length, length), 1)
    forget = [log_sigmoid(forget_ref[pl.ds(head_of(j, phase), 1), :]) for j in range(CORES)]
    running = lane_scan(padded(jnp.concatenate([reset_ref[...].astype(f32)] + forget, axis=0)))
    running_rows = running.T
    count, count_rows = running[0:1], running_rows[:, 0:1]
    linked = jnp.logical_and(count_rows == count, t_at >= s_at)
    for j in range(CORES):
        head = head_of(j, phase)
        query = (mine_ref, theirs_ref)[j][...]
        keys = k_ref[:, pl.ds(pl.multiple_of(head * size, size), size)]
        values = v_ref[:, pl.ds(pl.multiple_of(head * vsize, vsize), vsize)]
        base = pl.multiple_of(head * stride, EXTRA)
        memory = state[pl.ds(base, size), :]
        extra = state[pl.ds(pl.multiple_of(base + size, EXTRA), EXTRA), :].astype(f32)
        normer = (extra[0:1] + extra[1:2] + extra[2:3]).astype(bf16).astype(f32)
        top = extra[3:4, 0:1] + extra[4:5, 0:1] + extra[5:6, 0:1]
        top = jnp.where(place == 0, very_low, top)
        cum_t = running_rows[:, 1 + j : 2 + j]
        exponent = jnp.where(
            linked,
            cum_t - running[1 + j : 2 + j] + gate_ref[pl.ds(head, 1), :],
            very_low,
        )
        carried = jnp.where(count_rows == 0.0, cum_t + top, very_low)
        row_max = jnp.maximum(jnp.max(exponent, axis=1, keepdims=True), carried)
        scores = lax.dot_general(
            query, keys, (((1,), (1,)), ((), ())), preferred_element_type=f32
        )
        weighted = (jnp.exp(exponent - row_max) * (scores * factor)).astype(bf16)
        scale = jnp.exp(carried - row_max) * factor
        cross = jnp.dot(query, memory, preferred_element_type=f32)
        inter = jnp.sum(query.astype(f32) * normer, axis=1, keepdims=True)
        numerator = jnp.dot(weighted, values, preferred_element_type=f32) + scale * cross
        denominator = jnp.sum(weighted.astype(f32), axis=1, keepdims=True) + scale * inter
        floor = jnp.exp(jnp.maximum(-row_max, 0.0))
        hidden = (numerator / jnp.maximum(jnp.abs(denominator), floor)).astype(bf16)
        if phase < ng - 1:
            out_ref[:, j * vsize : (j + 1) * vsize] = hidden
        else:
            out_ref[:, pl.ds(pl.multiple_of(head * vsize, vsize), vsize)] = hidden
    if phase:
        for r in range(phase):
            for j in range(CORES):
                at = pl.multiple_of(head_of(j, r) * vsize, vsize)
                out_ref[:, pl.ds(at, vsize)] = earlier[:, j * vsize : (j + 1) * vsize]


VMEM = pl.BlockSpec(memory_space=pltpu.VMEM)
ANY = pl.BlockSpec(memory_space=pl.ANY)


def make_body(mesh):
    ng, nd, nz = (mesh.shape[a] for a in AXES)
    nx = nd // CORES

    def send(value, where):
        return lax.ppermute(value, AXES, moves(mesh, where))

    def body(normed_input, query_weight, key_vectors, value_vectors, input_gate, forget_gate, resets):
        sequences, length, features = normed_input.shape
        heads = input_gate.shape[1]
        columns = query_weight.shape[1]
        width = columns // (ng * CORES)
        size = columns // heads
        keys, values = key_vectors[0], value_vectors[0]
        gate, forget = input_gate[0], forget_gate[0]
        vwidth = values.shape[1]
        group = lax.axis_index("groups")
        dp = lax.axis_index("dp")
        core, x = dp % CORES, dp // CORES
        rows = query_weight.shape[0]
        half = columns // CORES
        depth = features // nx
        flat = normed_input[0]

        def columns_of(value, at, count):
            return lax.dynamic_slice_in_dim(value, at * count, count, 1)

        def over_core(value):
            return send(value, lambda g, x, k, z: (g, x, 1 - k, z))

        swapped = over_core(columns_of(query_weight, 1 - core, half))
        kept = columns_of(query_weight, core, half)
        parts = [
            jnp.stack([columns_of(v, (group + r) % ng, width) for v in (kept, swapped)])
            for r in range(ng)
        ]
        tokens = [columns_of(flat, x, depth)]
        away = [columns_of(flat, (x + rel) % nx, depth) for rel in range(1, nx)]
        arrived = [
            send(away[rel - 1], lambda g, x, k, z: (g, (x + rel) % nx, k, z))
            for rel in range(1, nx)
        ]
        tokens.append(over_core(tokens[0]))
        for value in arrived:
            tokens.extend([value, over_core(value)])
        pieces = [[parts[r]] for r in range(ng)]
        for s in range(1, nz):
            mine = send(parts[0], lambda g, x, k, z: (g, x, k, z ^ s))
            pieces[0].append(mine)
            for r in range(1, ng):
                pieces[r].append(send(mine, lambda g, x, k, z: ((g - r) % ng, x, k, z)))
        stride = size + EXTRA
        message = jax.ShapeDtypeStruct((heads * stride, vwidth // heads), bf16)
        own, first, side = pl.pallas_call(
            functools.partial(state_kernel, heads),
            out_shape=(
                jax.ShapeDtypeStruct((heads * size, vwidth // heads), f32),
                message,
                jax.ShapeDtypeStruct((heads * 8, vwidth // heads), f32),
            ),
            in_specs=[VMEM] * 5,
            out_specs=(VMEM,) * 3,
            name="own_state",
        )(keys, values, gate, forget, resets)
        states = []
        current = first
        for hop in range(1, nz):
            state = send(
                current, lambda g, x, k, z: (g, x, k, z + 1) if z == hop - 1 else None
            )
            states.append(state)
            if hop < nz - 1:
                current = pl.pallas_call(
                    functools.partial(combine_kernel, heads),
                    out_shape=message,
                    in_specs=[VMEM] * 3,
                    out_specs=VMEM,
                    name="combine",
                )(state, own, side)
        hidden = None
        for r in range(ng):
            sums, away = pl.pallas_call(
                functools.partial(project_kernel, nz, nx),
                out_shape=(
                    jax.ShapeDtypeStruct((CORES, length, width), f32),
                    jax.ShapeDtypeStruct((nx - 1, CORES, length, width), bf16),
                ),
                in_specs=[ANY] * (CORES * nx + nz),
                out_specs=(VMEM, VMEM),
                scratch_shapes=[
                    pltpu.VMEM((CORES * nx, length, depth), bf16),
                    pltpu.VMEM((depth, width), bf16),
                    pltpu.SemaphoreType.DMA((CORES * (nx + nz),)),
                ],
                name=f"project_{r}",
            )(*tokens, *pieces[r])
            total = sums
            for rel in range(1, nx):
                total = total + send(
                    away[rel - 1], lambda g, x, k, z: (g, (x - rel) % nx, k, z)
                ).astype(f32)
            total = total.astype(bf16)
            mine, theirs = total[0], over_core(total[1])
            hidden = pl.pallas_call(
                functools.partial(read_kernel, heads, len(states), r),
                out_shape=jax.ShapeDtypeStruct(
                    (length, vwidth if r == ng - 1 else CORES * (vwidth // heads)), bf16
                ),
                in_specs=[VMEM] * 7 + [ANY] * len(states) + [VMEM] * (1 if r else 0),
                out_specs=VMEM,
                scratch_shapes=[pltpu.VMEM(message.shape, bf16), pltpu.SemaphoreType.DMA(())],
                name=f"read_out_{r}",
            )(
                mine, theirs, keys, values, gate, forget, resets, *states,
                *([hidden] if r else []),
            )
        return hidden[None]

    return body


def solution(mesh):
    return jax.shard_map(
        make_body(mesh),
        mesh=mesh,
        in_specs=(
            P(("groups", "dp"), "ctx", None),
            P(("dp", "ctx"), None),
            P(("groups", "dp"), "ctx", None),
            P(("groups", "dp"), "ctx", None),
            P(("groups", "dp"), None, "ctx"),
            P(("groups", "dp"), None, "ctx"),
            P(("groups", "dp"), "ctx"),
        ),
        out_specs=P(("groups", "dp"), "ctx", None),
        check_vma=False,
    )
```

```python
import functools

import jax
import jax.numpy as jnp
from jax import lax
from jax.experimental import pallas as pl
from jax.experimental.pallas import tpu as pltpu
from jax.sharding import PartitionSpec as P


very_low = -1e30
AXES = ("groups", "dp", "ctx")
CORES = 2
EXTRA = 16
f32 = jnp.float32
bf16 = jnp.bfloat16


def moves(mesh, where):
    ng, nd, nz = (mesh.shape[a] for a in AXES)
    pairs = []
    for g in range(ng):
        for x in range(nd // CORES):
            for k in range(CORES):
                for z in range(nz):
                    to = where(g, x, k, z)
                    if to is not None:
                        g2, x2, k2, z2 = to
                        source = (g * nd + x * CORES + k) * nz + z
                        pairs.append((source, (g2 * nd + x2 * CORES + k2) * nz + z2))
    return pairs


def lane_scan(values):
    length = values.shape[1]
    lane = lax.broadcasted_iota(jnp.int32, values.shape, 1)
    step = 1
    while step < length:
        moved = pltpu.roll(values, step, 1)
        values = values + jnp.where(lane >= step, moved, jnp.zeros_like(values))
        step *= 2
    return values


def log_sigmoid(x):
    return jnp.minimum(x, 0.0) - jnp.log1p(jnp.exp(-jnp.abs(x)))


def padded(values):
    rows = values.shape[0]
    if rows % 8 == 0:
        return values
    fill = jnp.zeros((8 - rows % 8, values.shape[1]), values.dtype)
    return jnp.concatenate([values, fill], axis=0)


def split_rows(value):
    high = value.astype(bf16)
    rest = value - high.astype(f32)
    mid = rest.astype(bf16)
    low = (rest - mid.astype(f32)).astype(bf16)
    return high, mid, low


def store_message(out_ref, base, size, memory, normer, top):
    out_ref[base : base + size, :] = memory.astype(bf16)
    n_parts = split_rows(normer)
    t_parts = split_rows(jnp.broadcast_to(top, normer.shape))
    row = lax.broadcasted_iota(jnp.int32, (EXTRA, normer.shape[1]), 0)
    block = jnp.zeros((EXTRA, normer.shape[1]), f32)
    for i, part in enumerate(n_parts + t_parts):
        block = jnp.where(row == i, part.astype(f32), block)
    out_ref[base + size : base + size + EXTRA, :] = block.astype(bf16)


def load_message(ref, base, size):
    extra = ref[base + size : base + size + EXTRA, :].astype(f32)
    normer = extra[0:1] + extra[1:2] + extra[2:3]
    top = extra[3:4, 0:1] + extra[4:5, 0:1] + extra[5:6, 0:1]
    return ref[base : base + size, :], normer, top


def prepare_kernel(heads, ng, nx, *refs):
    k_ref, v_ref, x_ref, w_ref, gate_ref, forget_ref, reset_ref = refs[:7]
    wsend_ref, xown_ref = refs[7:9]
    xaway = refs[9 : 8 + nx]
    chunks = refs[8 + nx : 8 + nx + 3 * ng]
    kbuf, vbuf, sems = refs[8 + nx + 3 * ng :]
    length = k_ref.shape[0]
    size, vsize = k_ref.shape[1] // heads, v_ref.shape[1] // heads
    group, dp = lax.axis_index("groups"), lax.axis_index("dp")
    core, x = lax.rem(dp, CORES), lax.div(dp, CORES)
    half = wsend_ref.shape[1]
    depth = xown_ref.shape[1]

    def block(ref, at, count):
        return ref.at[:, pl.ds(pl.multiple_of(at * count, count), count)]

    moved = [
        (k_ref, kbuf),
        (v_ref, vbuf),
        (block(w_ref, 1 - core, half), wsend_ref),
    ]
    for rel in range(1, nx):
        moved.append((block(x_ref, lax.rem(x + rel, nx), depth), xaway[rel - 1]))
    moved.append((block(x_ref, x, depth), xown_ref))
    copies = []
    for i, (source, target) in enumerate(moved):
        copy = pltpu.make_async_copy(source, target, sems.at[i])
        copy.start()
        copies.append(copy)
    count = lane_scan(padded(reset_ref[...].astype(f32)))[0:1]
    cumulative = lane_scan(padded(log_sigmoid(forget_ref[...])))[0:heads]
    total = cumulative[:, length - 1 : length]
    final = count[:, length - 1 : length]
    expo = jnp.where(count == final, total - cumulative + gate_ref[...], very_low)
    top = jnp.max(expo, axis=1, keepdims=True)
    weight = padded(jnp.exp(expo - top)).T
    gap = jnp.where(final > 0, very_low, total)
    copies[0].wait()
    copies[1].wait()
    for r in range(ng):
        own_ref, msg_ref, side_ref = chunks[3 * r : 3 * r + 3]
        for j in range(heads // ng):
            within = lax.rem(group + r, ng)
            head = j * ng + within

            def pick(values):
                chosen = values[j * ng]
                for i in range(1, ng):
                    chosen = jnp.where(within == i, values[j * ng + i], chosen)
                return chosen

            keys = kbuf[:, pl.ds(pl.multiple_of(head * size, size), size)].astype(f32)
            values = vbuf[:, pl.ds(pl.multiple_of(head * vsize, vsize), vsize)]
            scale = pick([weight[:, h : h + 1] for h in range(heads)])
            this_top = pick([top[h : h + 1] for h in range(heads)])
            this_gap = pick([gap[h : h + 1] for h in range(heads)])
            weighted = (keys * scale).astype(bf16)
            memory = lax.dot_general(
                weighted, values, (((0,), (0,)), ((), ())), preferred_element_type=f32
            )
            normer = jnp.sum(weighted.astype(f32), axis=0, keepdims=True)
            own_ref[j * size : (j + 1) * size, :] = memory
            side_ref[j * 8 : j * 8 + 1, :] = normer
            side_ref[j * 8 + 1 : j * 8 + 2, :] = jnp.broadcast_to(this_top, normer.shape)
            side_ref[j * 8 + 2 : j * 8 + 3, :] = jnp.broadcast_to(this_gap, normer.shape)
            store_message(msg_ref, j * (size + EXTRA), size, memory, normer, this_top)
    for copy in copies[2:]:
        copy.wait()


def combine_kernel(heads, prev_ref, own_ref, side_ref, msg_ref):
    size = own_ref.shape[0] // heads
    stride = size + EXTRA
    for h in range(heads):
        memory, normer, top = load_message(prev_ref, h * stride, size)
        own_normer = side_ref[h * 8 : h * 8 + 1, :]
        own_top = side_ref[h * 8 + 1 : h * 8 + 2, 0:1]
        gap = side_ref[h * 8 + 2 : h * 8 + 3, 0:1]
        shifted = top + gap
        both = jnp.maximum(shifted, own_top)
        early = jnp.exp(shifted - both)
        late = jnp.exp(own_top - both)
        joined = early * memory.astype(f32) + late * own_ref[h * size : (h + 1) * size, :]
        store_message(msg_ref, h * stride, size, joined, early * normer + late * own_normer, both)


def project_kernel(nz, nx, *refs):
    count = CORES * nx
    blocks, parts = refs[:count], refs[count : count + nz]
    outs = refs[count + nz : 2 * count + nz]
    tokens, whole, sems = refs[2 * count + nz :]
    rows = parts[0].shape[1]
    place = lax.axis_index("ctx")
    core = lax.rem(lax.axis_index("dp"), CORES)
    copies = []
    for s in range(nz):
        source = place ^ s
        for j in range(CORES):
            owner = lax.rem(core + j, CORES)
            row = pl.multiple_of((owner * nz + source) * rows, rows)
            copies.append((parts[s].at[j], whole.at[pl.ds(row, rows)]))
    sequence = list(range(CORES, count)) + list(range(CORES))
    for i in sequence:
        copies.append((blocks[i], tokens.at[i]))
    started = []
    for i, (source, target) in enumerate(copies):
        copy = pltpu.make_async_copy(source, target, sems.at[i])
        copy.start()
        started.append(copy)
    for copy in started[: nz * CORES]:
        copy.wait()
    for at, i in enumerate(sequence):
        started[nz * CORES + at].wait()
        value = jnp.dot(tokens[i], whole[...], preferred_element_type=f32)
        outs[i][...] = value.astype(outs[i].dtype)


def read_kernel(heads, ng, nx, hops, phase, *refs):
    partials = [refs[j * nx : (j + 1) * nx] for j in range(CORES)]
    k_ref, v_ref, gate_ref, forget_ref, reset_ref = refs[CORES * nx : CORES * nx + 5]
    at = CORES * nx + 5
    done = phase if phase == ng - 1 else 0
    states, earlier = refs[at : at + hops], refs[at + hops : at + hops + done]
    out_ref, kbuf, vbuf, state, sems = refs[at + hops + done :]
    length = k_ref.shape[0]
    size, vsize = k_ref.shape[1] // heads, v_ref.shape[1] // heads
    factor = size ** (-0.5)
    stride = size + EXTRA
    group, dp, place = (lax.axis_index(a) for a in AXES)
    core = lax.rem(dp, CORES)

    def slot_of(j):
        return lax.rem(core + j, CORES)

    def head_of(j, r):
        return slot_of(j) * ng + lax.rem(group + r, ng)

    copies = []
    for j in range(CORES):
        head = head_of(j, phase)
        for i, (ref, buffer, wide) in enumerate(((k_ref, kbuf, size), (v_ref, vbuf, vsize))):
            source = ref.at[:, pl.ds(pl.multiple_of(head * wide, wide), wide)]
            copy = pltpu.make_async_copy(source, buffer.at[j], sems.at[2 * j + i])
            copy.start()
            copies.append(copy)
    for h in range(hops):

        @pl.when(place == h + 1)
        def _():
            pltpu.make_async_copy(states[h], state, sems.at[2 * CORES]).start()

    @pl.when(place == 0)
    def _():
        state[...] = jnp.zeros_like(state)

    t_at = lax.broadcasted_iota(jnp.int32, (length, length), 0)
    s_at = lax.broadcasted_iota(jnp.int32, (length, length), 1)
    forget = [log_sigmoid(forget_ref[pl.ds(head_of(j, phase), 1), :]) for j in range(CORES)]
    running = lane_scan(padded(jnp.concatenate([reset_ref[...].astype(f32)] + forget, axis=0)))
    running_rows = running.T
    count, count_rows = running[0:1], running_rows[:, 0:1]
    linked = jnp.logical_and(count_rows == count, t_at >= s_at)
    exponents = []
    for j in range(CORES):
        exponents.append(
            jnp.where(
                linked,
                running_rows[:, 1 + j : 2 + j]
                - running[1 + j : 2 + j]
                + gate_ref[pl.ds(head_of(j, phase), 1), :],
                very_low,
            )
        )

    @pl.when(place > 0)
    def _():
        pltpu.make_async_copy(states[0], state, sems.at[2 * CORES]).wait()

    for copy in copies:
        copy.wait()
    for j in range(CORES):
        total = partials[j][0][...]
        for other in partials[j][1:]:
            total = total + other[...].astype(f32)
        query = total.astype(bf16)
        keys, values = kbuf[j], vbuf[j]
        base = pl.multiple_of(slot_of(j) * stride, EXTRA)
        memory = state[pl.ds(base, size), :]
        extra = state[pl.ds(pl.multiple_of(base + size, EXTRA), EXTRA), :].astype(f32)
        normer = (extra[0:1] + extra[1:2] + extra[2:3]).astype(bf16).astype(f32)
        top = extra[3:4, 0:1] + extra[4:5, 0:1] + extra[5:6, 0:1]
        top = jnp.where(place == 0, very_low, top)
        exponent = exponents[j]
        carried = jnp.where(count_rows == 0.0, running_rows[:, 1 + j : 2 + j] + top, very_low)
        row_max = jnp.maximum(jnp.max(exponent, axis=1, keepdims=True), carried)
        scores = lax.dot_general(
            query, keys, (((1,), (1,)), ((), ())), preferred_element_type=f32
        )
        weighted = (jnp.exp(exponent - row_max) * (scores * factor)).astype(bf16)
        scale = jnp.exp(carried - row_max) * factor
        cross = jnp.dot(query, memory, preferred_element_type=f32)
        inter = jnp.sum(query.astype(f32) * normer, axis=1, keepdims=True)
        numerator = jnp.dot(weighted, values, preferred_element_type=f32) + scale * cross
        denominator = jnp.sum(weighted.astype(f32), axis=1, keepdims=True) + scale * inter
        floor = jnp.exp(jnp.maximum(-row_max, 0.0))
        hidden = (numerator / jnp.maximum(jnp.abs(denominator), floor)).astype(bf16)
        if phase < ng - 1:
            out_ref[:, j * vsize : (j + 1) * vsize] = hidden
        else:
            target = pl.multiple_of(head_of(j, phase) * vsize, vsize)
            out_ref[:, pl.ds(target, vsize)] = hidden
    if phase == ng - 1:
        for r in range(phase):
            for j in range(CORES):
                target = pl.multiple_of(head_of(j, r) * vsize, vsize)
                out_ref[:, pl.ds(target, vsize)] = earlier[r][:, j * vsize : (j + 1) * vsize]


VMEM = pl.BlockSpec(memory_space=pltpu.VMEM)
ANY = pl.BlockSpec(memory_space=pl.ANY)


def make_body(mesh):
    ng, nd, nz = (mesh.shape[a] for a in AXES)
    nx = nd // CORES

    def send(value, where):
        return lax.ppermute(value, AXES, moves(mesh, where))

    def over_core(value):
        return send(value, lambda g, x, k, z: (g, x, 1 - k, z))

    def call(kernel, *args, **options):
        return pl.pallas_call(kernel, **options)(*args)

    def body(normed_input, query_weight, key_vectors, value_vectors, input_gate, forget_gate, resets):
        _, length, features = normed_input.shape
        heads = input_gate.shape[1]
        columns = query_weight.shape[1]
        width = columns // (ng * CORES)
        size = columns // heads
        keys, values = key_vectors[0], value_vectors[0]
        gate, forget = input_gate[0], forget_gate[0]
        vwidth = values.shape[1]
        group = lax.axis_index("groups")
        dp = lax.axis_index("dp")
        core = dp % CORES
        half = columns // CORES
        depth = features // nx
        flat = normed_input[0]

        def columns_of(value, at, count):
            return lax.dynamic_slice_in_dim(value, at * count, count, 1)

        stride = size + EXTRA
        vsize = vwidth // heads
        slots = heads // ng
        message = jax.ShapeDtypeStruct((slots * stride, vsize), bf16)
        block = jax.ShapeDtypeStruct((length, depth), flat.dtype)
        prepared = call(
            functools.partial(prepare_kernel, heads, ng, nx),
            keys, values, flat, query_weight, gate, forget, resets,
            out_shape=(
                jax.ShapeDtypeStruct((query_weight.shape[0], half), query_weight.dtype),
                *[block] * nx,
                *[
                    jax.ShapeDtypeStruct((slots * size, vsize), f32),
                    message,
                    jax.ShapeDtypeStruct((slots * 8, vsize), f32),
                ]
                * ng,
            ),
            in_specs=[ANY] * 4 + [VMEM] * 3,
            out_specs=(ANY,) * (1 + nx) + (VMEM,) * (3 * ng),
            scratch_shapes=[
                pltpu.VMEM(keys.shape, bf16),
                pltpu.VMEM(values.shape, bf16),
                pltpu.SemaphoreType.DMA((3 + nx,)),
            ],
        )
        swapped = over_core(prepared[0])
        kept = columns_of(query_weight, core, half)
        parts = [
            jnp.stack([columns_of(v, (group + r) % ng, width) for v in (kept, swapped)])
            for r in range(ng)
        ]
        tokens = [prepared[1]]
        arrived = [
            send(prepared[1 + rel], lambda g, x, k, z: (g, (x + rel) % nx, k, z))
            for rel in range(1, nx)
        ]
        tokens.append(over_core(tokens[0]))
        for rel, value in enumerate(arrived):
            tokens.extend([value, over_core(value)])
        pieces = [[parts[r]] for r in range(ng)]
        for s in range(1, nz):
            mine = send(parts[0], lambda g, x, k, z: (g, x, k, z ^ s))
            pieces[0].append(mine)
            for r in range(1, ng):
                pieces[r].append(send(mine, lambda g, x, k, z: ((g - r) % ng, x, k, z)))
        states = [[] for _ in range(ng)]
        for r in range(ng):
            own, current, side = prepared[1 + nx + 3 * r : 4 + nx + 3 * r]
            for hop in range(1, nz):
                state = send(current, lambda g, x, k, z: (g, x, k, z + 1) if z == hop - 1 else None)
                states[r].append(state)
                if hop < nz - 1:
                    current = call(
                        functools.partial(combine_kernel, slots),
                        state, own, side,
                        out_shape=message,
                        in_specs=[VMEM] * 3,
                        out_specs=VMEM,
                    )
        results = []
        for r in range(ng):
            piece = jax.ShapeDtypeStruct((length, width), f32)
            small = jax.ShapeDtypeStruct((length, width), bf16)
            sums = call(
                functools.partial(project_kernel, nz, nx),
                *tokens, *pieces[r],
                out_shape=(piece,) * CORES + (small,) * (CORES * (nx - 1)),
                in_specs=[ANY] * (CORES * nx + nz),
                out_specs=(VMEM,) * (CORES * nx),
                scratch_shapes=[
                    pltpu.VMEM((CORES * nx, length, depth), bf16),
                    pltpu.VMEM((depth, width), bf16),
                    pltpu.SemaphoreType.DMA((CORES * (nx + nz),)),
                ],
            )
            partials = [[sums[0]], [over_core(sums[1])]]
            for rel in range(1, nx):
                for j in range(CORES):
                    partials[j].append(
                        send(
                            sums[CORES * rel + j], lambda g, x, k, z: (g, (x - rel) % nx, k ^ j, z)
                        )
                    )
            last = r == ng - 1
            results.append(
                call(
                    functools.partial(read_kernel, heads, ng, nx, nz - 1, r),
                    *partials[0], *partials[1], keys, values, gate, forget, resets,
                    *states[r], *(results if last else []),
                    out_shape=jax.ShapeDtypeStruct(
                        (length, vwidth if last else CORES * vsize), bf16
                    ),
                    in_specs=[VMEM] * (CORES * nx) + [ANY] * 2 + [VMEM] * 3
                    + [ANY] * (nz - 1) + [VMEM] * (r if last else 0),
                    out_specs=VMEM,
                    scratch_shapes=[
                        pltpu.VMEM((CORES, length, size), bf16),
                        pltpu.VMEM((CORES, length, vsize), bf16),
                        pltpu.VMEM(message.shape, bf16),
                        pltpu.SemaphoreType.DMA((2 * CORES + 1,)),
                    ],
                )
            )
        hidden = results[-1]
        return hidden[None]

    return body


def solution(mesh):
    return jax.shard_map(
        make_body(mesh),
        mesh=mesh,
        in_specs=(
            P(("groups", "dp"), "ctx", None),
            P(("dp", "ctx"), None),
            P(("groups", "dp"), "ctx", None),
            P(("groups", "dp"), "ctx", None),
            P(("groups", "dp"), None, "ctx"),
            P(("groups", "dp"), None, "ctx"),
            P(("groups", "dp"), "ctx"),
        ),
        out_specs=P(("groups", "dp"), "ctx", None),
        check_vma=False,
    )
```

```python
import functools

import jax
import jax.numpy as jnp
from jax import lax
from jax.experimental import pallas as pl
from jax.experimental.pallas import tpu as pltpu
from jax.sharding import PartitionSpec as P


very_low = -1e30
AXES = ("groups", "dp", "ctx")
CORES = 2
EXTRA = 16
f32 = jnp.float32
bf16 = jnp.bfloat16


def moves(mesh, where):
    ng, nd, nz = (mesh.shape[a] for a in AXES)
    pairs = []
    for g in range(ng):
        for x in range(nd // CORES):
            for k in range(CORES):
                for z in range(nz):
                    to = where(g, x, k, z)
                    if to is not None:
                        g2, x2, k2, z2 = to
                        source = (g * nd + x * CORES + k) * nz + z
                        pairs.append((source, (g2 * nd + x2 * CORES + k2) * nz + z2))
    return pairs


def lane_scan(values):
    length = values.shape[1]
    lane = lax.broadcasted_iota(jnp.int32, values.shape, 1)
    step = 1
    while step < length:
        moved = pltpu.roll(values, step, 1)
        values = values + jnp.where(lane >= step, moved, jnp.zeros_like(values))
        step *= 2
    return values


def log_sigmoid(x):
    return jnp.minimum(x, 0.0) - jnp.log1p(jnp.exp(-jnp.abs(x)))


def padded(values):
    rows = values.shape[0]
    if rows % 8 == 0:
        return values
    fill = jnp.zeros((8 - rows % 8, values.shape[1]), values.dtype)
    return jnp.concatenate([values, fill], axis=0)


def split_rows(value):
    high = value.astype(bf16)
    rest = value - high.astype(f32)
    mid = rest.astype(bf16)
    low = (rest - mid.astype(f32)).astype(bf16)
    return high, mid, low


def store_message(out_ref, base, size, memory, normer, top):
    out_ref[base : base + size, :] = memory.astype(bf16)
    n_parts = split_rows(normer)
    t_parts = split_rows(jnp.broadcast_to(top, normer.shape))
    row = lax.broadcasted_iota(jnp.int32, (EXTRA, normer.shape[1]), 0)
    block = jnp.zeros((EXTRA, normer.shape[1]), f32)
    for i, part in enumerate(n_parts + t_parts):
        block = jnp.where(row == i, part.astype(f32), block)
    out_ref[base + size : base + size + EXTRA, :] = block.astype(bf16)


def load_message(ref, base, size):
    extra = ref[base + size : base + size + EXTRA, :].astype(f32)
    normer = extra[0:1] + extra[1:2] + extra[2:3]
    top = extra[3:4, 0:1] + extra[4:5, 0:1] + extra[5:6, 0:1]
    return ref[base : base + size, :], normer, top


def prepare_kernel(heads, ng, nx, *refs):
    k_ref, v_ref, x_ref, w_ref, gate_ref, forget_ref, reset_ref = refs[:7]
    wsend_ref, xown_ref = refs[7:9]
    xaway = refs[9 : 8 + nx]
    chunks = refs[8 + nx : 8 + nx + 3 * ng]
    kbuf, vbuf, wbuf, xbuf, sems, out_sems = refs[8 + nx + 3 * ng :]
    length = k_ref.shape[0]
    size, vsize = k_ref.shape[1] // heads, v_ref.shape[1] // heads
    group, dp = lax.axis_index("groups"), lax.axis_index("dp")
    core, x = lax.rem(dp, CORES), lax.div(dp, CORES)
    half = wsend_ref.shape[1]
    depth = xown_ref.shape[1]

    def block(ref, at, count):
        return ref.at[:, pl.ds(pl.multiple_of(at * count, count), count)]

    moved = [
        (k_ref, kbuf),
        (v_ref, vbuf),
        (block(w_ref, 1 - core, half), wbuf),
    ]
    for rel in range(nx):
        moved.append((block(x_ref, lax.rem(x + rel, nx), depth), xbuf.at[rel]))
    copies = []
    for i, (source, target) in enumerate(moved):
        copy = pltpu.make_async_copy(source, target, sems.at[i])
        copy.start()
        copies.append(copy)
    count = lane_scan(padded(reset_ref[...].astype(f32)))[0:1]
    cumulative = lane_scan(padded(log_sigmoid(forget_ref[...])))[0:heads]
    total = cumulative[:, length - 1 : length]
    final = count[:, length - 1 : length]
    expo = jnp.where(count == final, total - cumulative + gate_ref[...], very_low)
    top = jnp.max(expo, axis=1, keepdims=True)
    weight = padded(jnp.exp(expo - top)).T
    gap = jnp.where(final > 0, very_low, total)
    leaving = [(wbuf, wsend_ref), (xbuf.at[0], xown_ref)]
    leaving += [(xbuf.at[rel], xaway[rel - 1]) for rel in range(1, nx)]
    for copy in copies:
        copy.wait()
    copies = []
    for i, (source, target) in enumerate(leaving):
        copy = pltpu.make_async_copy(source, target, out_sems.at[i])
        copy.start()
        copies.append(copy)
    for r in range(ng):
        own_ref, msg_ref, side_ref = chunks[3 * r : 3 * r + 3]
        for j in range(heads // ng):
            within = lax.rem(group + r, ng)
            head = j * ng + within

            def pick(values):
                chosen = values[j * ng]
                for i in range(1, ng):
                    chosen = jnp.where(within == i, values[j * ng + i], chosen)
                return chosen

            keys = kbuf[:, pl.ds(pl.multiple_of(head * size, size), size)].astype(f32)
            values = vbuf[:, pl.ds(pl.multiple_of(head * vsize, vsize), vsize)]
            scale = pick([weight[:, h : h + 1] for h in range(heads)])
            this_top = pick([top[h : h + 1] for h in range(heads)])
            this_gap = pick([gap[h : h + 1] for h in range(heads)])
            weighted = (keys * scale).astype(bf16)
            memory = lax.dot_general(
                weighted, values, (((0,), (0,)), ((), ())), preferred_element_type=f32
            )
            normer = jnp.sum(weighted.astype(f32), axis=0, keepdims=True)
            own_ref[j * size : (j + 1) * size, :] = memory
            side_ref[j * 8 : j * 8 + 1, :] = normer
            side_ref[j * 8 + 1 : j * 8 + 2, :] = jnp.broadcast_to(this_top, normer.shape)
            side_ref[j * 8 + 2 : j * 8 + 3, :] = jnp.broadcast_to(this_gap, normer.shape)
            store_message(msg_ref, j * (size + EXTRA), size, memory, normer, this_top)
    for copy in copies:
        copy.wait()


def combine_kernel(heads, prev_ref, own_ref, side_ref, msg_ref):
    size = own_ref.shape[0] // heads
    stride = size + EXTRA
    for h in range(heads):
        memory, normer, top = load_message(prev_ref, h * stride, size)
        own_normer = side_ref[h * 8 : h * 8 + 1, :]
        own_top = side_ref[h * 8 + 1 : h * 8 + 2, 0:1]
        gap = side_ref[h * 8 + 2 : h * 8 + 3, 0:1]
        shifted = top + gap
        both = jnp.maximum(shifted, own_top)
        early = jnp.exp(shifted - both)
        late = jnp.exp(own_top - both)
        joined = early * memory.astype(f32) + late * own_ref[h * size : (h + 1) * size, :]
        store_message(msg_ref, h * stride, size, joined, early * normer + late * own_normer, both)


def project_kernel(nz, nx, *refs):
    count = CORES * nx
    blocks, parts = refs[:count], refs[count : count + nz]
    outs = refs[count + nz : 2 * count + nz]
    tokens, whole, sems = refs[2 * count + nz :]
    rows = parts[0].shape[1]
    place = lax.axis_index("ctx")
    core = lax.rem(lax.axis_index("dp"), CORES)
    copies = []
    for s in range(nz):
        source = place ^ s
        for j in range(CORES):
            owner = lax.rem(core + j, CORES)
            row = pl.multiple_of((owner * nz + source) * rows, rows)
            copies.append((parts[s].at[j], whole.at[pl.ds(row, rows)]))
    sequence = list(range(CORES, count)) + list(range(CORES))
    for i in sequence:
        copies.append((blocks[i], tokens.at[i]))
    started = []
    for i, (source, target) in enumerate(copies):
        copy = pltpu.make_async_copy(source, target, sems.at[i])
        copy.start()
        started.append(copy)
    for copy in started[: nz * CORES]:
        copy.wait()
    for at, i in enumerate(sequence):
        started[nz * CORES + at].wait()
        value = jnp.dot(tokens[i], whole[...], preferred_element_type=f32)
        outs[i][...] = value.astype(outs[i].dtype)


def read_kernel(heads, ng, nx, hops, phase, *refs):
    partials = [refs[j * nx : (j + 1) * nx] for j in range(CORES)]
    k_ref, v_ref, gate_ref, forget_ref, reset_ref = refs[CORES * nx : CORES * nx + 5]
    at = CORES * nx + 5
    done = phase if phase == ng - 1 else 0
    states, earlier = refs[at : at + hops], refs[at + hops : at + hops + done]
    out_ref, kbuf, vbuf, state, sems = refs[at + hops + done :]
    length = k_ref.shape[0]
    size, vsize = k_ref.shape[1] // heads, v_ref.shape[1] // heads
    factor = size ** (-0.5)
    stride = size + EXTRA
    group, dp, place = (lax.axis_index(a) for a in AXES)
    core = lax.rem(dp, CORES)

    def slot_of(j):
        return lax.rem(core + j, CORES)

    def head_of(j, r):
        return slot_of(j) * ng + lax.rem(group + r, ng)

    copies = []
    for j in range(CORES):
        head = head_of(j, phase)
        for i, (ref, buffer, wide) in enumerate(((k_ref, kbuf, size), (v_ref, vbuf, vsize))):
            source = ref.at[:, pl.ds(pl.multiple_of(head * wide, wide), wide)]
            copy = pltpu.make_async_copy(source, buffer.at[j], sems.at[2 * j + i])
            copy.start()
            copies.append(copy)
    for h in range(hops):

        @pl.when(place == h + 1)
        def _():
            pltpu.make_async_copy(states[h], state, sems.at[2 * CORES]).start()

    @pl.when(place == 0)
    def _():
        state[...] = jnp.zeros_like(state)

    t_at = lax.broadcasted_iota(jnp.int32, (length, length), 0)
    s_at = lax.broadcasted_iota(jnp.int32, (length, length), 1)
    forget = [log_sigmoid(forget_ref[pl.ds(head_of(j, phase), 1), :]) for j in range(CORES)]
    running = lane_scan(padded(jnp.concatenate([reset_ref[...].astype(f32)] + forget, axis=0)))
    running_rows = running.T
    count, count_rows = running[0:1], running_rows[:, 0:1]
    linked = jnp.logical_and(count_rows == count, t_at >= s_at)
    exponents = []
    for j in range(CORES):
        exponents.append(
            jnp.where(
                linked,
                running_rows[:, 1 + j : 2 + j]
                - running[1 + j : 2 + j]
                + gate_ref[pl.ds(head_of(j, phase), 1), :],
                very_low,
            )
        )

    @pl.when(place > 0)
    def _():
        pltpu.make_async_copy(states[0], state, sems.at[2 * CORES]).wait()

    for copy in copies:
        copy.wait()
    for j in range(CORES):
        total = partials[j][0][...]
        for other in partials[j][1:]:
            total = total + other[...].astype(f32)
        query = total.astype(bf16)
        keys, values = kbuf[j], vbuf[j]
        base = pl.multiple_of(slot_of(j) * stride, EXTRA)
        memory = state[pl.ds(base, size), :]
        extra = state[pl.ds(pl.multiple_of(base + size, EXTRA), EXTRA), :].astype(f32)
        normer = (extra[0:1] + extra[1:2] + extra[2:3]).astype(bf16).astype(f32)
        top = extra[3:4, 0:1] + extra[4:5, 0:1] + extra[5:6, 0:1]
        top = jnp.where(place == 0, very_low, top)
        exponent = exponents[j]
        carried = jnp.where(count_rows == 0.0, running_rows[:, 1 + j : 2 + j] + top, very_low)
        row_max = jnp.maximum(jnp.max(exponent, axis=1, keepdims=True), carried)
        scores = lax.dot_general(
            query, keys, (((1,), (1,)), ((), ())), preferred_element_type=f32
        )
        weighted = (jnp.exp(exponent - row_max) * (scores * factor)).astype(bf16)
        scale = jnp.exp(carried - row_max) * factor
        cross = jnp.dot(query, memory, preferred_element_type=f32)
        inter = jnp.sum(query.astype(f32) * normer, axis=1, keepdims=True)
        numerator = jnp.dot(weighted, values, preferred_element_type=f32) + scale * cross
        denominator = jnp.sum(weighted.astype(f32), axis=1, keepdims=True) + scale * inter
        floor = jnp.exp(jnp.maximum(-row_max, 0.0))
        hidden = (numerator / jnp.maximum(jnp.abs(denominator), floor)).astype(bf16)
        if phase < ng - 1:
            out_ref[:, j * vsize : (j + 1) * vsize] = hidden
        else:
            target = pl.multiple_of(head_of(j, phase) * vsize, vsize)
            out_ref[:, pl.ds(target, vsize)] = hidden
    if phase == ng - 1:
        for r in range(phase):
            for j in range(CORES):
                target = pl.multiple_of(head_of(j, r) * vsize, vsize)
                out_ref[:, pl.ds(target, vsize)] = earlier[r][:, j * vsize : (j + 1) * vsize]


VMEM = pl.BlockSpec(memory_space=pltpu.VMEM)
ANY = pl.BlockSpec(memory_space=pl.ANY)


def make_body(mesh):
    ng, nd, nz = (mesh.shape[a] for a in AXES)
    nx = nd // CORES

    def send(value, where):
        return lax.ppermute(value, AXES, moves(mesh, where))

    def over_core(value):
        return send(value, lambda g, x, k, z: (g, x, 1 - k, z))

    def call(kernel, *args, **options):
        params = pltpu.CompilerParams(vmem_limit_bytes=20 * 2**20)
        return pl.pallas_call(kernel, compiler_params=params, **options)(*args)

    def body(normed_input, query_weight, key_vectors, value_vectors, input_gate, forget_gate, resets):
        _, length, features = normed_input.shape
        heads = input_gate.shape[1]
        columns = query_weight.shape[1]
        width = columns // (ng * CORES)
        size = columns // heads
        keys, values = key_vectors[0], value_vectors[0]
        gate, forget = input_gate[0], forget_gate[0]
        vwidth = values.shape[1]
        group = lax.axis_index("groups")
        dp = lax.axis_index("dp")
        core = dp % CORES
        half = columns // CORES
        depth = features // nx
        flat = normed_input[0]

        def columns_of(value, at, count):
            return lax.dynamic_slice_in_dim(value, at * count, count, 1)

        stride = size + EXTRA
        vsize = vwidth // heads
        slots = heads // ng
        message = jax.ShapeDtypeStruct((slots * stride, vsize), bf16)
        block = jax.ShapeDtypeStruct((length, depth), flat.dtype)
        prepared = call(
            functools.partial(prepare_kernel, heads, ng, nx),
            keys, values, flat, query_weight, gate, forget, resets,
            out_shape=(
                jax.ShapeDtypeStruct((query_weight.shape[0], half), query_weight.dtype),
                *[block] * nx,
                *[
                    jax.ShapeDtypeStruct((slots * size, vsize), f32),
                    message,
                    jax.ShapeDtypeStruct((slots * 8, vsize), f32),
                ]
                * ng,
            ),
            in_specs=[ANY] * 4 + [VMEM] * 3,
            out_specs=(ANY,) * (1 + nx) + (VMEM,) * (3 * ng),
            scratch_shapes=[
                pltpu.VMEM(keys.shape, bf16),
                pltpu.VMEM(values.shape, bf16),
                pltpu.VMEM((query_weight.shape[0], half), bf16),
                pltpu.VMEM((nx, length, depth), bf16),
                pltpu.SemaphoreType.DMA((3 + nx,)),
                pltpu.SemaphoreType.DMA((1 + nx,)),
            ],
        )
        swapped = over_core(prepared[0])
        kept = columns_of(query_weight, core, half)
        parts = [
            jnp.stack([columns_of(v, (group + r) % ng, width) for v in (kept, swapped)])
            for r in range(ng)
        ]
        tokens = [prepared[1]]
        arrived = [
            send(prepared[1 + rel], lambda g, x, k, z: (g, (x + rel) % nx, k, z))
            for rel in range(1, nx)
        ]
        tokens.append(over_core(tokens[0]))
        for rel, value in enumerate(arrived):
            tokens.extend([value, over_core(value)])
        pieces = [[parts[r]] for r in range(ng)]
        for s in range(1, nz):
            mine = send(parts[0], lambda g, x, k, z: (g, x, k, z ^ s))
            pieces[0].append(mine)
            for r in range(1, ng):
                pieces[r].append(send(mine, lambda g, x, k, z: ((g - r) % ng, x, k, z)))
        states = [[] for _ in range(ng)]
        for r in range(ng):
            own, current, side = prepared[1 + nx + 3 * r : 4 + nx + 3 * r]
            for hop in range(1, nz):
                state = send(current, lambda g, x, k, z: (g, x, k, z + 1) if z == hop - 1 else None)
                states[r].append(state)
                if hop < nz - 1:
                    current = call(
                        functools.partial(combine_kernel, slots),
                        state, own, side,
                        out_shape=message,
                        in_specs=[VMEM] * 3,
                        out_specs=VMEM,
                    )
        results = []
        for r in range(ng):
            piece = jax.ShapeDtypeStruct((length, width), f32)
            small = jax.ShapeDtypeStruct((length, width), bf16)
            sums = call(
                functools.partial(project_kernel, nz, nx),
                *tokens, *pieces[r],
                out_shape=(piece,) * CORES + (small,) * (CORES * (nx - 1)),
                in_specs=[ANY] * (CORES * nx + nz),
                out_specs=(VMEM,) * (CORES * nx),
                scratch_shapes=[
                    pltpu.VMEM((CORES * nx, length, depth), bf16),
                    pltpu.VMEM((depth, width), bf16),
                    pltpu.SemaphoreType.DMA((CORES * (nx + nz),)),
                ],
            )
            partials = [[sums[0]], [over_core(sums[1])]]
            for rel in range(1, nx):
                for j in range(CORES):
                    partials[j].append(
                        send(
                            sums[CORES * rel + j], lambda g, x, k, z: (g, (x - rel) % nx, k ^ j, z)
                        )
                    )
            last = r == ng - 1
            results.append(
                call(
                    functools.partial(read_kernel, heads, ng, nx, nz - 1, r),
                    *partials[0], *partials[1], keys, values, gate, forget, resets,
                    *states[r], *(results if last else []),
                    out_shape=jax.ShapeDtypeStruct(
                        (length, vwidth if last else CORES * vsize), bf16
                    ),
                    in_specs=[VMEM] * (CORES * nx) + [ANY] * 2 + [VMEM] * 3
                    + [ANY] * (nz - 1) + [VMEM] * (r if last else 0),
                    out_specs=VMEM,
                    scratch_shapes=[
                        pltpu.VMEM((CORES, length, size), bf16),
                        pltpu.VMEM((CORES, length, vsize), bf16),
                        pltpu.VMEM(message.shape, bf16),
                        pltpu.SemaphoreType.DMA((2 * CORES + 1,)),
                    ],
                )
            )
        hidden = results[-1]
        return hidden[None]

    return body


def solution(mesh):
    return jax.shard_map(
        make_body(mesh),
        mesh=mesh,
        in_specs=(
            P(("groups", "dp"), "ctx", None),
            P(("dp", "ctx"), None),
            P(("groups", "dp"), "ctx", None),
            P(("groups", "dp"), "ctx", None),
            P(("groups", "dp"), None, "ctx"),
            P(("groups", "dp"), None, "ctx"),
            P(("groups", "dp"), "ctx"),
        ),
        out_specs=P(("groups", "dp"), "ctx", None),
        check_vma=False,
    )
```

```python
import functools

import jax
import jax.numpy as jnp
from jax import lax
from jax.experimental import pallas as pl
from jax.experimental.pallas import tpu as pltpu
from jax.sharding import PartitionSpec as P


very_low = -1e30
AXES = ("groups", "dp", "ctx")
CORES = 2
EXTRA = 16
f32 = jnp.float32
bf16 = jnp.bfloat16


def moves(mesh, where):
    ng, nd, nz = (mesh.shape[a] for a in AXES)
    pairs = []
    for g in range(ng):
        for x in range(nd // CORES):
            for k in range(CORES):
                for z in range(nz):
                    to = where(g, x, k, z)
                    if to is not None:
                        g2, x2, k2, z2 = to
                        source = (g * nd + x * CORES + k) * nz + z
                        pairs.append((source, (g2 * nd + x2 * CORES + k2) * nz + z2))
    return pairs


def lane_scan(values):
    length = values.shape[1]
    lane = lax.broadcasted_iota(jnp.int32, values.shape, 1)
    step = 1
    while step < length:
        moved = pltpu.roll(values, step, 1)
        values = values + jnp.where(lane >= step, moved, jnp.zeros_like(values))
        step *= 2
    return values


def log_sigmoid(x):
    return jnp.minimum(x, 0.0) - jnp.log1p(jnp.exp(-jnp.abs(x)))


def padded(values):
    rows = values.shape[0]
    if rows % 8 == 0:
        return values
    fill = jnp.zeros((8 - rows % 8, values.shape[1]), values.dtype)
    return jnp.concatenate([values, fill], axis=0)


def split_rows(value):
    high = value.astype(bf16)
    rest = value - high.astype(f32)
    mid = rest.astype(bf16)
    low = (rest - mid.astype(f32)).astype(bf16)
    return high, mid, low


def store_message(out_ref, base, size, memory, normer, top):
    out_ref[base : base + size, :] = memory.astype(bf16)
    n_parts = split_rows(normer)
    t_parts = split_rows(jnp.broadcast_to(top, normer.shape))
    row = lax.broadcasted_iota(jnp.int32, (EXTRA, normer.shape[1]), 0)
    block = jnp.zeros((EXTRA, normer.shape[1]), f32)
    for i, part in enumerate(n_parts + t_parts):
        block = jnp.where(row == i, part.astype(f32), block)
    out_ref[base + size : base + size + EXTRA, :] = block.astype(bf16)


def load_message(ref, base, size):
    extra = ref[base + size : base + size + EXTRA, :].astype(f32)
    normer = extra[0:1] + extra[1:2] + extra[2:3]
    top = extra[3:4, 0:1] + extra[4:5, 0:1] + extra[5:6, 0:1]
    return ref[base : base + size, :], normer, top


def slice_kernel(ng, nx, x_ref, w_ref, send_ref, *refs):
    own, away, sems = refs[:ng], refs[ng : ng + nx - 1], refs[ng + nx - 1]
    group, dp = lax.axis_index("groups"), lax.axis_index("dp")
    core, x = lax.rem(dp, CORES), lax.div(dp, CORES)
    half, width, depth = send_ref.shape[1], own[0].shape[1], away[0].shape[1]
    copies = []

    def copy(ref, column, target):
        source = ref.at[:, pl.ds(pl.multiple_of(column, width), target.shape[1])]
        copies.append(pltpu.make_async_copy(source, target, sems.at[len(copies)]))
        copies[-1].start()

    copy(w_ref, (1 - core) * half, send_ref)
    for r in range(ng):
        copy(w_ref, core * half + lax.rem(group + r, ng) * width, own[r])
    for rel in range(1, nx):
        copy(x_ref, lax.rem(x + rel, nx) * depth, away[rel - 1])
    for each in copies:
        each.wait()


def pack_kernel(own_ref, swapped_ref, out_ref):
    _, width = own_ref.shape
    column = pl.multiple_of(lax.axis_index("groups") * width, width)
    out_ref[0] = own_ref[...]
    out_ref[1] = swapped_ref[:, pl.ds(column, width)]


def state_kernel(heads, ng, *refs):
    k_ref, v_ref, x_ref, gate_ref, forget_ref, reset_ref, xown_ref = refs[:7]
    chunks, sem = refs[7 : 7 + 3 * ng], refs[7 + 3 * ng]
    length = k_ref.shape[0]
    size, vsize = k_ref.shape[1] // heads, v_ref.shape[1] // heads
    group, dp = lax.axis_index("groups"), lax.axis_index("dp")
    depth = xown_ref.shape[1]
    column = pl.multiple_of(lax.div(dp, CORES) * depth, depth)
    copy = pltpu.make_async_copy(x_ref.at[:, pl.ds(column, depth)], xown_ref, sem)
    copy.start()
    count = lane_scan(padded(reset_ref[...].astype(f32)))[0:1]
    cumulative = lane_scan(padded(log_sigmoid(forget_ref[...])))[0:heads]
    total = cumulative[:, length - 1 : length]
    final = count[:, length - 1 : length]
    expo = jnp.where(count == final, total - cumulative + gate_ref[...], very_low)
    top = jnp.max(expo, axis=1, keepdims=True)
    weight = padded(jnp.exp(expo - top)).T
    gap = jnp.where(final > 0, very_low, total)
    for r in range(ng):
        own_ref, msg_ref, side_ref = chunks[3 * r : 3 * r + 3]
        for j in range(heads // ng):
            within = lax.rem(group + r, ng)
            head = j * ng + within

            def pick(values):
                chosen = values[j * ng]
                for i in range(1, ng):
                    chosen = jnp.where(within == i, values[j * ng + i], chosen)
                return chosen

            keys = k_ref[:, pl.ds(pl.multiple_of(head * size, size), size)].astype(f32)
            values = v_ref[:, pl.ds(pl.multiple_of(head * vsize, vsize), vsize)]
            scale = pick([weight[:, h : h + 1] for h in range(heads)])
            this_top = pick([top[h : h + 1] for h in range(heads)])
            this_gap = pick([gap[h : h + 1] for h in range(heads)])
            weighted = (keys * scale).astype(bf16)
            memory = lax.dot_general(
                weighted, values, (((0,), (0,)), ((), ())), preferred_element_type=f32
            )
            normer = jnp.sum(weighted.astype(f32), axis=0, keepdims=True)
            own_ref[j * size : (j + 1) * size, :] = memory
            side_ref[j * 8 : j * 8 + 1, :] = normer
            side_ref[j * 8 + 1 : j * 8 + 2, :] = jnp.broadcast_to(this_top, normer.shape)
            side_ref[j * 8 + 2 : j * 8 + 3, :] = jnp.broadcast_to(this_gap, normer.shape)
            store_message(msg_ref, j * (size + EXTRA), size, memory, normer, this_top)
    copy.wait()


def combine_kernel(heads, prev_ref, own_ref, side_ref, msg_ref):
    size = own_ref.shape[0] // heads
    stride = size + EXTRA
    for h in range(heads):
        memory, normer, top = load_message(prev_ref, h * stride, size)
        own_normer = side_ref[h * 8 : h * 8 + 1, :]
        own_top = side_ref[h * 8 + 1 : h * 8 + 2, 0:1]
        gap = side_ref[h * 8 + 2 : h * 8 + 3, 0:1]
        shifted = top + gap
        both = jnp.maximum(shifted, own_top)
        early = jnp.exp(shifted - both)
        late = jnp.exp(own_top - both)
        joined = early * memory.astype(f32) + late * own_ref[h * size : (h + 1) * size, :]
        store_message(msg_ref, h * stride, size, joined, early * normer + late * own_normer, both)


def away_kernel(nz, ng, phase, count, *refs):
    split = nz == 4
    first = 2 if phase else 1
    tokens, parts = refs[:count], refs[count : count + first + nz - 1 + split]
    outs, whole = refs[count + len(parts) : -1], refs[-1]
    rows, width = parts[-1].shape[1:]
    place, group = lax.axis_index("ctx"), lax.axis_index("groups")
    core = lax.rem(lax.axis_index("dp"), CORES)
    if phase:
        column = pl.multiple_of(lax.rem(group + phase, ng) * width, width)
        values = [(parts[0][...], parts[1][:, pl.ds(column, width)])]
    else:
        values = [(parts[0][0], parts[0][1])]
    steps = list(range(nz))
    for part in parts[first:]:
        values.append((part[0], part[1]))
    if split:
        inner = jnp.logical_or(place == 1, place == 2)
        outer = values.pop()
        values[-1] = tuple(jnp.where(inner, a, b) for a, b in zip(values[-1], outer))
        steps = [0, 2, 1, 3]
    for at, s in enumerate(steps):
        for j in range(CORES):
            owner = lax.rem(core + j, CORES)
            row = pl.multiple_of((owner * nz + (place ^ s)) * rows, rows)
            whole[pl.ds(row, rows), :] = values[at][j]
    for token, out in zip(tokens, outs):
        value = jnp.dot(token[...], whole[...], preferred_element_type=f32)
        out[...] = value.astype(out.dtype)


def keep_kernel(*refs):
    tokens, whole, outs = refs[:CORES], refs[CORES], refs[CORES + 1 :]
    for token, out in zip(tokens, outs):
        out[...] = jnp.dot(token[...], whole[...], preferred_element_type=f32)


def read_kernel(heads, ng, nx, hops, phase, *refs):
    partials = [refs[j * nx : (j + 1) * nx] for j in range(CORES)]
    k_ref, v_ref, gate_ref, forget_ref, reset_ref = refs[CORES * nx : CORES * nx + 5]
    at = CORES * nx + 5
    done = phase if phase == ng - 1 else 0
    states, earlier = refs[at : at + hops], refs[at + hops : at + hops + done]
    out_ref, state, sem = refs[at + hops + done :]
    length = k_ref.shape[0]
    size, vsize = k_ref.shape[1] // heads, v_ref.shape[1] // heads
    factor = size ** (-0.5)
    stride = size + EXTRA
    group, dp, place = (lax.axis_index(a) for a in AXES)
    core = lax.rem(dp, CORES)

    def slot_of(j):
        return lax.rem(core + j, CORES)

    def head_of(j, r):
        return slot_of(j) * ng + lax.rem(group + r, ng)

    for h in range(hops):

        @pl.when(place == h + 1)
        def _():
            pltpu.make_async_copy(states[h], state, sem).start()

    @pl.when(place == 0)
    def _():
        state[...] = jnp.zeros_like(state)

    t_at = lax.broadcasted_iota(jnp.int32, (length, length), 0)
    s_at = lax.broadcasted_iota(jnp.int32, (length, length), 1)
    forget = [log_sigmoid(forget_ref[pl.ds(head_of(j, phase), 1), :]) for j in range(CORES)]
    running = lane_scan(padded(jnp.concatenate([reset_ref[...].astype(f32)] + forget, axis=0)))
    running_rows = running.T
    count, count_rows = running[0:1], running_rows[:, 0:1]
    linked = jnp.logical_and(count_rows == count, t_at >= s_at)
    exponents = []
    for j in range(CORES):
        exponents.append(
            jnp.where(
                linked,
                running_rows[:, 1 + j : 2 + j]
                - running[1 + j : 2 + j]
                + gate_ref[pl.ds(head_of(j, phase), 1), :],
                very_low,
            )
        )

    @pl.when(place > 0)
    def _():
        pltpu.make_async_copy(states[0], state, sem).wait()

    for j in range(CORES):
        total = partials[j][0][...]
        for other in partials[j][1:]:
            total = total + other[...].astype(f32)
        query = total.astype(bf16)
        head = head_of(j, phase)
        keys = k_ref[:, pl.ds(pl.multiple_of(head * size, size), size)]
        values = v_ref[:, pl.ds(pl.multiple_of(head * vsize, vsize), vsize)]
        base = pl.multiple_of(slot_of(j) * stride, EXTRA)
        memory = state[pl.ds(base, size), :]
        extra = state[pl.ds(pl.multiple_of(base + size, EXTRA), EXTRA), :].astype(f32)
        normer = (extra[0:1] + extra[1:2] + extra[2:3]).astype(bf16).astype(f32)
        top = extra[3:4, 0:1] + extra[4:5, 0:1] + extra[5:6, 0:1]
        top = jnp.where(place == 0, very_low, top)
        exponent = exponents[j]
        carried = jnp.where(count_rows == 0.0, running_rows[:, 1 + j : 2 + j] + top, very_low)
        row_max = jnp.maximum(jnp.max(exponent, axis=1, keepdims=True), carried)
        scores = lax.dot_general(
            query, keys, (((1,), (1,)), ((), ())), preferred_element_type=f32
        )
        weighted = (jnp.exp(exponent - row_max) * (scores * factor)).astype(bf16)
        scale = jnp.exp(carried - row_max) * factor
        cross = jnp.dot(query, memory, preferred_element_type=f32)
        inter = jnp.sum(query.astype(f32) * normer, axis=1, keepdims=True)
        numerator = jnp.dot(weighted, values, preferred_element_type=f32) + scale * cross
        denominator = jnp.sum(weighted.astype(f32), axis=1, keepdims=True) + scale * inter
        floor = jnp.exp(jnp.maximum(-row_max, 0.0))
        hidden = (numerator / jnp.maximum(jnp.abs(denominator), floor)).astype(bf16)
        if phase < ng - 1:
            out_ref[:, j * vsize : (j + 1) * vsize] = hidden
        else:
            target = pl.multiple_of(head_of(j, phase) * vsize, vsize)
            out_ref[:, pl.ds(target, vsize)] = hidden
    if phase == ng - 1:
        for r in range(phase):
            for j in range(CORES):
                target = pl.multiple_of(head_of(j, r) * vsize, vsize)
                out_ref[:, pl.ds(target, vsize)] = earlier[r][:, j * vsize : (j + 1) * vsize]


VMEM = pl.BlockSpec(memory_space=pltpu.VMEM)
ANY = pl.BlockSpec(memory_space=pl.ANY)


def gather_plan(nz):
    if nz != 4:
        return [(s, None, lambda z, s=s: z ^ s) for s in range(1, nz)]
    return [
        ("2", None, lambda z: z ^ 2),
        ("1", None, lambda z: z ^ 1),
        ("in", None, lambda z: z ^ 3 if z in (1, 2) else None),
        ("out", "2", lambda z: {1: 0, 2: 3}.get(z)),
    ]


def make_body(mesh):
    ng, nd, nz = (mesh.shape[a] for a in AXES)
    nx = nd // CORES

    def send(value, where):
        return lax.ppermute(value, AXES, moves(mesh, where))

    def over_core(value):
        return send(value, lambda g, x, k, z: (g, x, 1 - k, z))

    def call(kernel, *args, **options):
        params = pltpu.CompilerParams(vmem_limit_bytes=20 * 2**20)
        return pl.pallas_call(kernel, compiler_params=params, **options)(*args)

    def body(normed_input, query_weight, key_vectors, value_vectors, input_gate, forget_gate, resets):
        _, length, features = normed_input.shape
        heads = input_gate.shape[1]
        columns = query_weight.shape[1]
        width = columns // (ng * CORES)
        size = columns // heads
        keys, values = key_vectors[0], value_vectors[0]
        gate, forget = input_gate[0], forget_gate[0]
        vwidth = values.shape[1]
        half = columns // CORES
        depth = features // nx
        flat = normed_input[0]

        stride = size + EXTRA
        vsize = vwidth // heads
        slots = heads // ng
        message = jax.ShapeDtypeStruct((slots * stride, vsize), bf16)
        block = jax.ShapeDtypeStruct((length, depth), flat.dtype)
        hbm_tokens = pltpu.with_memory_space_constraint(flat, pltpu.HBM)
        hbm_weight = pltpu.with_memory_space_constraint(query_weight, pltpu.HBM)
        rows = query_weight.shape[0]
        quarter = jax.ShapeDtypeStruct((rows, width), query_weight.dtype)
        sliced = call(
            functools.partial(slice_kernel, ng, nx),
            hbm_tokens, hbm_weight,
            out_shape=(
                jax.ShapeDtypeStruct((rows, half), query_weight.dtype),
                *[quarter] * ng,
                *[block] * (nx - 1),
            ),
            in_specs=[ANY] * 2,
            out_specs=(VMEM,) * (ng + nx),
            scratch_shapes=[pltpu.SemaphoreType.DMA((ng + nx,))],
        )
        swapped = over_core(sliced[0])
        own_parts = sliced[1 : 1 + ng]
        arrived = [
            send(sliced[ng + rel], lambda g, x, k, z: (g, (x + rel) % nx, k, z))
            for rel in range(1, nx)
        ]
        packed = call(
            pack_kernel,
            own_parts[0], swapped,
            out_shape=jax.ShapeDtypeStruct((CORES, rows, width), bf16),
            in_specs=[VMEM] * 2,
            out_specs=VMEM,
        )
        prepared = call(
            functools.partial(state_kernel, heads, ng),
            keys, values, hbm_tokens, gate, forget, resets,
            out_shape=(
                block,
                *[
                    jax.ShapeDtypeStruct((slots * size, vsize), f32),
                    message,
                    jax.ShapeDtypeStruct((slots * 8, vsize), f32),
                ]
                * ng,
            ),
            in_specs=[VMEM] * 2 + [ANY] + [VMEM] * 3,
            out_specs=(VMEM,) * (1 + 3 * ng),
            scratch_shapes=[pltpu.SemaphoreType.DMA(())],
        )
        tokens = [prepared[0]]
        tokens.append(over_core(tokens[0]))
        for rel, value in enumerate(arrived):
            tokens.extend([value, over_core(value)])
        pieces = [[packed]] + [[own_parts[r], swapped] for r in range(1, ng)]
        gathered = {}
        for name, origin, where in gather_plan(nz):
            value = packed if origin is None else gathered[origin]
            mine = send(value, lambda g, x, k, z: None if where(z) is None else (g, x, k, where(z)))
            gathered[name] = mine
            pieces[0].append(mine)
            for r in range(1, ng):
                pieces[r].append(
                    send(
                        mine,
                        lambda g, x, k, z: (
                            ((g - r) % ng, x, k, z) if z in map(where, range(nz)) else None
                        ),
                    )
                )
        states = [[] for _ in range(ng)]
        for r in range(ng):
            own, current, side = prepared[1 + 3 * r : 4 + 3 * r]
            for hop in range(1, nz):
                state = send(current, lambda g, x, k, z: (g, x, k, z + 1) if z == hop - 1 else None)
                states[r].append(state)
                if hop < nz - 1:
                    current = call(
                        functools.partial(combine_kernel, slots),
                        state, own, side,
                        out_shape=message,
                        in_specs=[VMEM] * 3,
                        out_specs=VMEM,
                    )
        results = []
        for r in range(ng):
            piece = jax.ShapeDtypeStruct((length, width), f32)
            small = jax.ShapeDtypeStruct((length, width), bf16)
            count = CORES * (nx - 1)
            sent = call(
                functools.partial(away_kernel, nz, ng, r, count),
                *tokens[CORES:], *pieces[r],
                out_shape=(small,) * count + (jax.ShapeDtypeStruct((depth, width), bf16),),
                in_specs=[VMEM] * (count + len(pieces[r])),
                out_specs=(VMEM,) * (count + 1),
            )
            kept = call(
                keep_kernel,
                *tokens[:CORES], sent[-1],
                out_shape=(piece,) * CORES,
                in_specs=[VMEM] * (CORES + 1),
                out_specs=(VMEM,) * CORES,
            )
            sums = [*kept, *sent[:-1]]
            partials = [[sums[0]], [over_core(sums[1])]]
            for rel in range(1, nx):
                for j in range(CORES):
                    partials[j].append(
                        send(
                            sums[CORES * rel + j], lambda g, x, k, z: (g, (x - rel) % nx, k ^ j, z)
                        )
                    )
            last = r == ng - 1
            results.append(
                call(
                    functools.partial(read_kernel, heads, ng, nx, nz - 1, r),
                    *partials[0], *partials[1], keys, values, gate, forget, resets,
                    *states[r], *(results if last else []),
                    out_shape=jax.ShapeDtypeStruct(
                        (length, vwidth if last else CORES * vsize), bf16
                    ),
                    in_specs=[VMEM] * (CORES * nx + 5)
                    + [ANY] * (nz - 1) + [VMEM] * (r if last else 0),
                    out_specs=VMEM,
                    scratch_shapes=[
                        pltpu.VMEM(message.shape, bf16),
                        pltpu.SemaphoreType.DMA(()),
                    ],
                )
            )
        hidden = results[-1]
        return hidden[None]

    return body


def solution(mesh):
    return jax.shard_map(
        make_body(mesh),
        mesh=mesh,
        in_specs=(
            P(("groups", "dp"), "ctx", None),
            P(("dp", "ctx"), None),
            P(("groups", "dp"), "ctx", None),
            P(("groups", "dp"), "ctx", None),
            P(("groups", "dp"), None, "ctx"),
            P(("groups", "dp"), None, "ctx"),
            P(("groups", "dp"), "ctx"),
        ),
        out_specs=P(("groups", "dp"), "ctx", None),
        check_vma=False,
    )
```

```python
import functools

import jax
import jax.numpy as jnp
from jax import lax
from jax.experimental import pallas as pl
from jax.experimental.pallas import tpu as pltpu
from jax.sharding import PartitionSpec as P


very_low = -1e30
AXES = ("groups", "dp", "ctx")
CORES = 2
EXTRA = 16
f32 = jnp.float32
bf16 = jnp.bfloat16


def moves(mesh, where):
    ng, nd, nz = (mesh.shape[a] for a in AXES)
    pairs = []
    for g in range(ng):
        for x in range(nd // CORES):
            for k in range(CORES):
                for z in range(nz):
                    to = where(g, x, k, z)
                    if to is not None:
                        g2, x2, k2, z2 = to
                        source = (g * nd + x * CORES + k) * nz + z
                        pairs.append((source, (g2 * nd + x2 * CORES + k2) * nz + z2))
    return pairs


def lane_scan(values):
    length = values.shape[1]
    lane = lax.broadcasted_iota(jnp.int32, values.shape, 1)
    step = 1
    while step < length:
        moved = pltpu.roll(values, step, 1)
        values = values + jnp.where(lane >= step, moved, jnp.zeros_like(values))
        step *= 2
    return values


def log_sigmoid(x):
    return jnp.minimum(x, 0.0) - jnp.log1p(jnp.exp(-jnp.abs(x)))


def padded(values):
    rows = values.shape[0]
    if rows % 8 == 0:
        return values
    fill = jnp.zeros((8 - rows % 8, values.shape[1]), values.dtype)
    return jnp.concatenate([values, fill], axis=0)


def split_rows(value):
    high = value.astype(bf16)
    rest = value - high.astype(f32)
    mid = rest.astype(bf16)
    low = (rest - mid.astype(f32)).astype(bf16)
    return high, mid, low


def store_message(out_ref, base, size, memory, normer, top):
    out_ref[base : base + size, :] = memory.astype(bf16)
    n_parts = split_rows(normer)
    t_parts = split_rows(jnp.broadcast_to(top, normer.shape))
    row = lax.broadcasted_iota(jnp.int32, (EXTRA, normer.shape[1]), 0)
    block = jnp.zeros((EXTRA, normer.shape[1]), f32)
    for i, part in enumerate(n_parts + t_parts):
        block = jnp.where(row == i, part.astype(f32), block)
    out_ref[base + size : base + size + EXTRA, :] = block.astype(bf16)


def load_message(ref, base, size):
    extra = ref[base + size : base + size + EXTRA, :].astype(f32)
    normer = extra[0:1] + extra[1:2] + extra[2:3]
    top = extra[3:4, 0:1] + extra[4:5, 0:1] + extra[5:6, 0:1]
    return ref[base : base + size, :], normer, top


def slice_kernel(ng, nx, x_ref, w_ref, send_ref, *refs):
    own, away, sems = refs[:ng], refs[ng : ng + nx - 1], refs[ng + nx - 1]
    group, dp = lax.axis_index("groups"), lax.axis_index("dp")
    core, x = lax.rem(dp, CORES), lax.div(dp, CORES)
    half, width, depth = send_ref.shape[1], own[0].shape[1], away[0].shape[1]
    copies = []

    def copy(ref, column, target):
        source = ref.at[:, pl.ds(pl.multiple_of(column, width), target.shape[1])]
        copies.append(pltpu.make_async_copy(source, target, sems.at[len(copies)]))
        copies[-1].start()

    copy(w_ref, (1 - core) * half, send_ref)
    for r in range(ng):
        copy(w_ref, core * half + lax.rem(group + r, ng) * width, own[r])
    for rel in range(1, nx):
        copy(x_ref, lax.rem(x + rel, nx) * depth, away[rel - 1])
    for each in copies:
        each.wait()


def pack_kernel(own_ref, swapped_ref, out_ref):
    _, width = own_ref.shape
    column = pl.multiple_of(lax.axis_index("groups") * width, width)
    out_ref[0] = own_ref[...]
    out_ref[1] = swapped_ref[:, pl.ds(column, width)]


def state_kernel(heads, ng, *refs):
    k_ref, v_ref, x_ref, gate_ref, forget_ref, reset_ref, xown_ref = refs[:7]
    chunks, sem = refs[7 : 7 + 3 * ng], refs[7 + 3 * ng]
    length = k_ref.shape[0]
    size, vsize = k_ref.shape[1] // heads, v_ref.shape[1] // heads
    group, dp = lax.axis_index("groups"), lax.axis_index("dp")
    depth = xown_ref.shape[1]
    column = pl.multiple_of(lax.div(dp, CORES) * depth, depth)
    copy = pltpu.make_async_copy(x_ref.at[:, pl.ds(column, depth)], xown_ref, sem)
    copy.start()
    count = lane_scan(padded(reset_ref[...].astype(f32)))[0:1]
    cumulative = lane_scan(padded(log_sigmoid(forget_ref[...])))[0:heads]
    total = cumulative[:, length - 1 : length]
    final = count[:, length - 1 : length]
    expo = jnp.where(count == final, total - cumulative + gate_ref[...], very_low)
    top = jnp.max(expo, axis=1, keepdims=True)
    weight = padded(jnp.exp(expo - top)).T
    gap = jnp.where(final > 0, very_low, total)
    for r in range(ng):
        own_ref, msg_ref, side_ref = chunks[3 * r : 3 * r + 3]
        for j in range(heads // ng):
            within = lax.rem(group + r, ng)
            head = j * ng + within

            def pick(values):
                chosen = values[j * ng]
                for i in range(1, ng):
                    chosen = jnp.where(within == i, values[j * ng + i], chosen)
                return chosen

            keys = k_ref[:, pl.ds(pl.multiple_of(head * size, size), size)].astype(f32)
            values = v_ref[:, pl.ds(pl.multiple_of(head * vsize, vsize), vsize)]
            scale = pick([weight[:, h : h + 1] for h in range(heads)])
            this_top = pick([top[h : h + 1] for h in range(heads)])
            this_gap = pick([gap[h : h + 1] for h in range(heads)])
            weighted = (keys * scale).astype(bf16)
            memory = lax.dot_general(
                weighted, values, (((0,), (0,)), ((), ())), preferred_element_type=f32
            )
            normer = jnp.sum(weighted.astype(f32), axis=0, keepdims=True)
            own_ref[j * size : (j + 1) * size, :] = memory
            side_ref[j * 8 : j * 8 + 1, :] = normer
            side_ref[j * 8 + 1 : j * 8 + 2, :] = jnp.broadcast_to(this_top, normer.shape)
            side_ref[j * 8 + 2 : j * 8 + 3, :] = jnp.broadcast_to(this_gap, normer.shape)
            store_message(msg_ref, j * (size + EXTRA), size, memory, normer, this_top)
    copy.wait()


def join(slots, prev_ref, own_ref, side_ref, out_ref):
    size = own_ref.shape[0] // slots
    stride = size + EXTRA
    for h in range(slots):
        memory, normer, top = load_message(prev_ref, h * stride, size)
        own_normer = side_ref[h * 8 : h * 8 + 1, :]
        own_top = side_ref[h * 8 + 1 : h * 8 + 2, 0:1]
        gap = side_ref[h * 8 + 2 : h * 8 + 3, 0:1]
        shifted = top + gap
        both = jnp.maximum(shifted, own_top)
        early = jnp.exp(shifted - both)
        late = jnp.exp(own_top - both)
        joined = early * memory.astype(f32) + late * own_ref[h * size : (h + 1) * size, :]
        normers = early * normer + late * own_normer
        store_message(out_ref, h * stride, size, joined, normers, both)


def combine_kernel(slots, sender, prev_ref, own_ref, side_ref, out_ref):
    place = lax.axis_index("ctx")

    @pl.when(place == sender)
    def _():
        join(slots, prev_ref, own_ref, side_ref, out_ref)

    @pl.when(place != sender)
    def _():
        out_ref[...] = prev_ref[...]


def mix_kernel(message_ref, piece_ref, out_ref):
    place = lax.axis_index("ctx")
    rows = piece_ref.shape[1]

    @pl.when(place == 0)
    def _():
        out_ref[...] = message_ref[...]

    @pl.when(place != 0)
    def _():
        for j in range(CORES):
            out_ref[j * rows : (j + 1) * rows, :] = piece_ref[j]
        rest = out_ref.shape[0] - CORES * rows
        out_ref[CORES * rows :, :] = jnp.zeros((rest, out_ref.shape[1]), out_ref.dtype)


def pick_kernel(inner_ref, outer_ref, out_ref):
    place = lax.axis_index("ctx")
    rows = out_ref.shape[1]
    inner = jnp.logical_or(place == 1, place == 2)

    @pl.when(inner)
    def _():
        out_ref[...] = inner_ref[...]

    @pl.when(jnp.logical_not(inner))
    def _():
        for j in range(CORES):
            out_ref[j] = outer_ref[j * rows : (j + 1) * rows, :]


def away_kernel(nz, ng, phase, count, *refs):
    first = 2 if phase else 1
    tokens, parts = refs[:count], refs[count : count + first + nz - 1]
    outs, whole = refs[count + len(parts) : -1], refs[-1]
    rows, width = parts[-1].shape[1:]
    place, group = lax.axis_index("ctx"), lax.axis_index("groups")
    core = lax.rem(lax.axis_index("dp"), CORES)
    if phase:
        column = pl.multiple_of(lax.rem(group + phase, ng) * width, width)
        values = [(parts[0][...], parts[1][:, pl.ds(column, width)])]
    else:
        values = [(parts[0][0], parts[0][1])]
    for part in parts[first:]:
        values.append((part[0], part[1]))
    for s in range(nz):
        for j in range(CORES):
            owner = lax.rem(core + j, CORES)
            row = pl.multiple_of((owner * nz + (place ^ s)) * rows, rows)
            whole[pl.ds(row, rows), :] = values[s][j]
    for token, out in zip(tokens, outs):
        value = jnp.dot(token[...], whole[...], preferred_element_type=f32)
        out[...] = value.astype(out.dtype)


def keep_kernel(*refs):
    tokens, whole, outs = refs[:CORES], refs[CORES], refs[CORES + 1 :]
    for token, out in zip(tokens, outs):
        out[...] = jnp.dot(token[...], whole[...], preferred_element_type=f32)


def read_kernel(heads, ng, nx, hops, phase, *refs):
    partials = [refs[j * nx : (j + 1) * nx] for j in range(CORES)]
    k_ref, v_ref, gate_ref, forget_ref, reset_ref = refs[CORES * nx : CORES * nx + 5]
    at = CORES * nx + 5
    done = phase if phase == ng - 1 else 0
    states, earlier = refs[at : at + hops], refs[at + hops : at + hops + done]
    out_ref, state, sem = refs[at + hops + done :]
    length = k_ref.shape[0]
    size, vsize = k_ref.shape[1] // heads, v_ref.shape[1] // heads
    factor = size ** (-0.5)
    stride = size + EXTRA
    group, dp, place = (lax.axis_index(a) for a in AXES)
    core = lax.rem(dp, CORES)

    def slot_of(j):
        return lax.rem(core + j, CORES)

    def head_of(j, r):
        return slot_of(j) * ng + lax.rem(group + r, ng)

    for h in range(hops):

        @pl.when(place == h + 1)
        def _():
            pltpu.make_async_copy(states[h], state, sem).start()

    @pl.when(place == 0)
    def _():
        state[...] = jnp.zeros_like(state)

    t_at = lax.broadcasted_iota(jnp.int32, (length, length), 0)
    s_at = lax.broadcasted_iota(jnp.int32, (length, length), 1)
    forget = [log_sigmoid(forget_ref[pl.ds(head_of(j, phase), 1), :]) for j in range(CORES)]
    running = lane_scan(padded(jnp.concatenate([reset_ref[...].astype(f32)] + forget, axis=0)))
    running_rows = running.T
    count, count_rows = running[0:1], running_rows[:, 0:1]
    linked = jnp.logical_and(count_rows == count, t_at >= s_at)
    exponents = []
    for j in range(CORES):
        exponents.append(
            jnp.where(
                linked,
                running_rows[:, 1 + j : 2 + j]
                - running[1 + j : 2 + j]
                + gate_ref[pl.ds(head_of(j, phase), 1), :],
                very_low,
            )
        )

    @pl.when(place > 0)
    def _():
        pltpu.make_async_copy(states[0], state, sem).wait()

    for j in range(CORES):
        total = partials[j][0][...]
        for other in partials[j][1:]:
            total = total + other[...].astype(f32)
        query = total.astype(bf16)
        head = head_of(j, phase)
        keys = k_ref[:, pl.ds(pl.multiple_of(head * size, size), size)]
        values = v_ref[:, pl.ds(pl.multiple_of(head * vsize, vsize), vsize)]
        base = pl.multiple_of(slot_of(j) * stride, EXTRA)
        memory = state[pl.ds(base, size), :]
        extra = state[pl.ds(pl.multiple_of(base + size, EXTRA), EXTRA), :].astype(f32)
        normer = (extra[0:1] + extra[1:2] + extra[2:3]).astype(bf16).astype(f32)
        top = extra[3:4, 0:1] + extra[4:5, 0:1] + extra[5:6, 0:1]
        top = jnp.where(place == 0, very_low, top)
        exponent = exponents[j]
        carried = jnp.where(count_rows == 0.0, running_rows[:, 1 + j : 2 + j] + top, very_low)
        row_max = jnp.maximum(jnp.max(exponent, axis=1, keepdims=True), carried)
        scores = lax.dot_general(
            query, keys, (((1,), (1,)), ((), ())), preferred_element_type=f32
        )
        weighted = (jnp.exp(exponent - row_max) * (scores * factor)).astype(bf16)
        scale = jnp.exp(carried - row_max) * factor
        cross = jnp.dot(query, memory, preferred_element_type=f32)
        inter = jnp.sum(query.astype(f32) * normer, axis=1, keepdims=True)
        numerator = jnp.dot(weighted, values, preferred_element_type=f32) + scale * cross
        denominator = jnp.sum(weighted.astype(f32), axis=1, keepdims=True) + scale * inter
        floor = jnp.exp(jnp.maximum(-row_max, 0.0))
        hidden = (numerator / jnp.maximum(jnp.abs(denominator), floor)).astype(bf16)
        if phase < ng - 1:
            out_ref[:, j * vsize : (j + 1) * vsize] = hidden
        else:
            target = pl.multiple_of(head_of(j, phase) * vsize, vsize)
            out_ref[:, pl.ds(target, vsize)] = hidden
    if phase == ng - 1:
        for r in range(phase):
            for j in range(CORES):
                target = pl.multiple_of(head_of(j, r) * vsize, vsize)
                out_ref[:, pl.ds(target, vsize)] = earlier[r][:, j * vsize : (j + 1) * vsize]


VMEM = pl.BlockSpec(memory_space=pltpu.VMEM)
ANY = pl.BlockSpec(memory_space=pl.ANY)


def links(z):
    return {z: z + 1, z + 1: z}


def compact(mesh):
    return mesh.shape["ctx"] == 4 and mesh.shape["groups"] == CORES == 2


def make_body(mesh):
    ng, nd, nz = (mesh.shape[a] for a in AXES)
    nx = nd // CORES

    def send(value, where):
        return lax.ppermute(value, AXES, moves(mesh, where))

    def over_core(value):
        return send(value, lambda g, x, k, z: (g, x, 1 - k, z))

    def call(kernel, *args, **options):
        params = pltpu.CompilerParams(vmem_limit_bytes=20 * 2**20)
        return pl.pallas_call(kernel, compiler_params=params, **options)(*args)

    def body(normed_input, query_weight, key_vectors, value_vectors, input_gate, forget_gate, resets):
        _, length, features = normed_input.shape
        heads = input_gate.shape[1]
        columns = query_weight.shape[1]
        width = columns // (ng * CORES)
        size = columns // heads
        keys, values = key_vectors[0], value_vectors[0]
        gate, forget = input_gate[0], forget_gate[0]
        vwidth = values.shape[1]
        half = columns // CORES
        depth = features // nx
        flat = normed_input[0]

        stride = size + EXTRA
        vsize = vwidth // heads
        slots = heads // ng
        message = jax.ShapeDtypeStruct((slots * stride, vsize), bf16)
        block = jax.ShapeDtypeStruct((length, depth), flat.dtype)
        hbm_tokens = pltpu.with_memory_space_constraint(flat, pltpu.HBM)
        hbm_weight = pltpu.with_memory_space_constraint(query_weight, pltpu.HBM)
        rows = query_weight.shape[0]
        quarter = jax.ShapeDtypeStruct((rows, width), query_weight.dtype)
        sliced = call(
            functools.partial(slice_kernel, ng, nx),
            hbm_tokens, hbm_weight,
            out_shape=(
                jax.ShapeDtypeStruct((rows, half), query_weight.dtype),
                *[quarter] * ng,
                *[block] * (nx - 1),
            ),
            in_specs=[ANY] * 2,
            out_specs=(VMEM,) * (ng + nx),
            scratch_shapes=[pltpu.SemaphoreType.DMA((ng + nx,))],
        )
        swapped = over_core(sliced[0])
        own_parts = sliced[1 : 1 + ng]
        arrived = [
            send(sliced[ng + rel], lambda g, x, k, z: (g, (x + rel) % nx, k, z))
            for rel in range(1, nx)
        ]
        packed = call(
            pack_kernel,
            own_parts[0], swapped,
            out_shape=jax.ShapeDtypeStruct((CORES, rows, width), bf16),
            in_specs=[VMEM] * 2,
            out_specs=VMEM,
        )
        prepared = call(
            functools.partial(state_kernel, heads, ng),
            keys, values, hbm_tokens, gate, forget, resets,
            out_shape=(
                block,
                *[
                    jax.ShapeDtypeStruct((slots * size, vsize), f32),
                    message,
                    jax.ShapeDtypeStruct((slots * 8, vsize), f32),
                ]
                * ng,
            ),
            in_specs=[VMEM] * 2 + [ANY] + [VMEM] * 3,
            out_specs=(VMEM,) * (1 + 3 * ng),
            scratch_shapes=[pltpu.SemaphoreType.DMA(())],
        )
        tokens = [prepared[0]]
        tokens.append(over_core(tokens[0]))
        for rel, value in enumerate(arrived):
            tokens.extend([value, over_core(value)])
        pieces = [[packed]] + [[own_parts[r], swapped] for r in range(1, ng)]

        def over_ctx(value, targets):
            return send(
                value,
                lambda g, x, k, z: (g, x, k, targets[z]) if z in targets else (g, x, 1 - k, z),
            )

        own = [prepared[1 + 3 * r] for r in range(ng)]
        first = [prepared[2 + 3 * r] for r in range(ng)]
        side = [prepared[3 + 3 * r] for r in range(ng)]
        states = [[over_ctx(first[0], links(0))]] + [[] for _ in range(1, ng)]

        def extend(hop, r):
            message_out = call(
                functools.partial(combine_kernel, slots, hop - 1),
                states[r][-1], own[r], side[r],
                out_shape=message,
                in_specs=[VMEM] * 3,
                out_specs=VMEM,
            )
            states[r].append(over_ctx(message_out, links(hop - 1)))

        gathered = {
            s: over_ctx(packed, {z: z ^ s for z in range(nz)})
            for s in (range(1, nz) if not compact(mesh) else (2, 1))
        }
        if compact(mesh):
            inside = over_ctx(packed, links(1))
            mixed = call(
                mix_kernel,
                first[1], gathered[2],
                out_shape=message,
                in_specs=[VMEM] * 2,
                out_specs=VMEM,
            )
            outside = over_ctx(mixed, {**links(0), **links(2)})
            states[1].append(outside)
            gathered[3] = call(
                pick_kernel,
                inside, outside,
                out_shape=jax.ShapeDtypeStruct(packed.shape, bf16),
                in_specs=[VMEM] * 2,
                out_specs=VMEM,
            )
        else:
            for r in range(1, ng):
                states[r].append(over_ctx(first[r], links(0)))
        for hop in range(2, nz):
            for r in range(ng):
                extend(hop, r)
        for s in range(1, nz):
            pieces[0].append(gathered[s])
            for r in range(1, ng):
                pieces[r].append(send(gathered[s], lambda g, x, k, z: ((g - r) % ng, x, k, z)))
        results = []
        for r in range(ng):
            piece = jax.ShapeDtypeStruct((length, width), f32)
            small = jax.ShapeDtypeStruct((length, width), bf16)
            count = CORES * (nx - 1)
            sent = call(
                functools.partial(away_kernel, nz, ng, r, count),
                *tokens[CORES:], *pieces[r],
                out_shape=(small,) * count + (jax.ShapeDtypeStruct((depth, width), bf16),),
                in_specs=[VMEM] * (count + len(pieces[r])),
                out_specs=(VMEM,) * (count + 1),
            )
            kept = call(
                keep_kernel,
                *tokens[:CORES], sent[-1],
                out_shape=(piece,) * CORES,
                in_specs=[VMEM] * (CORES + 1),
                out_specs=(VMEM,) * CORES,
            )
            sums = [*kept, *sent[:-1]]
            partials = [[sums[0]], [over_core(sums[1])]]
            for rel in range(1, nx):
                for j in range(CORES):
                    partials[j].append(
                        send(
                            sums[CORES * rel + j], lambda g, x, k, z: (g, (x - rel) % nx, k ^ j, z)
                        )
                    )
            last = r == ng - 1
            results.append(
                call(
                    functools.partial(read_kernel, heads, ng, nx, nz - 1, r),
                    *partials[0], *partials[1], keys, values, gate, forget, resets,
                    *states[r], *(results if last else []),
                    out_shape=jax.ShapeDtypeStruct(
                        (length, vwidth if last else CORES * vsize), bf16
                    ),
                    in_specs=[VMEM] * (CORES * nx + 5)
                    + [ANY] * (nz - 1) + [VMEM] * (r if last else 0),
                    out_specs=VMEM,
                    scratch_shapes=[
                        pltpu.VMEM(message.shape, bf16),
                        pltpu.SemaphoreType.DMA(()),
                    ],
                )
            )
        hidden = results[-1]
        return hidden[None]

    return body


def solution(mesh):
    return jax.shard_map(
        make_body(mesh),
        mesh=mesh,
        in_specs=(
            P(("groups", "dp"), "ctx", None),
            P(("dp", "ctx"), None),
            P(("groups", "dp"), "ctx", None),
            P(("groups", "dp"), "ctx", None),
            P(("groups", "dp"), None, "ctx"),
            P(("groups", "dp"), None, "ctx"),
            P(("groups", "dp"), "ctx"),
        ),
        out_specs=P(("groups", "dp"), "ctx", None),
        check_vma=False,
    )
```

```python
import functools

import jax
import jax.numpy as jnp
from jax import lax
from jax.experimental import pallas as pl
from jax.experimental.pallas import tpu as pltpu
from jax.sharding import PartitionSpec as P


very_low = -1e30
AXES = ("groups", "dp", "ctx")
CORES = 2
EXTRA = 16
f32 = jnp.float32
bf16 = jnp.bfloat16


def moves(mesh, where):
    ng, nd, nz = (mesh.shape[a] for a in AXES)
    pairs = []
    for g in range(ng):
        for x in range(nd // CORES):
            for k in range(CORES):
                for z in range(nz):
                    to = where(g, x, k, z)
                    if to is not None:
                        g2, x2, k2, z2 = to
                        source = (g * nd + x * CORES + k) * nz + z
                        pairs.append((source, (g2 * nd + x2 * CORES + k2) * nz + z2))
    return pairs


def lane_scan(values):
    length = values.shape[1]
    lane = lax.broadcasted_iota(jnp.int32, values.shape, 1)
    step = 1
    while step < length:
        moved = pltpu.roll(values, step, 1)
        values = values + jnp.where(lane >= step, moved, jnp.zeros_like(values))
        step *= 2
    return values


def log_sigmoid(x):
    return jnp.minimum(x, 0.0) - jnp.log1p(jnp.exp(-jnp.abs(x)))


def padded(values):
    rows = values.shape[0]
    if rows % 8 == 0:
        return values
    fill = jnp.zeros((8 - rows % 8, values.shape[1]), values.dtype)
    return jnp.concatenate([values, fill], axis=0)


def split_rows(value):
    high = value.astype(bf16)
    rest = value - high.astype(f32)
    mid = rest.astype(bf16)
    low = (rest - mid.astype(f32)).astype(bf16)
    return high, mid, low


def store_message(out_ref, base, size, memory, normer, top):
    out_ref[base : base + size, :] = memory.astype(bf16)
    n_parts = split_rows(normer)
    t_parts = split_rows(jnp.broadcast_to(top, normer.shape))
    row = lax.broadcasted_iota(jnp.int32, (EXTRA, normer.shape[1]), 0)
    block = jnp.zeros((EXTRA, normer.shape[1]), f32)
    for i, part in enumerate(n_parts + t_parts):
        block = jnp.where(row == i, part.astype(f32), block)
    out_ref[base + size : base + size + EXTRA, :] = block.astype(bf16)


def load_message(ref, base, size):
    extra = ref[base + size : base + size + EXTRA, :].astype(f32)
    normer = extra[0:1] + extra[1:2] + extra[2:3]
    top = extra[3:4, 0:1] + extra[4:5, 0:1] + extra[5:6, 0:1]
    return ref[base : base + size, :], normer, top


def slice_kernel(ng, nx, x_ref, w_ref, send_ref, *refs):
    own, away, sems = refs[:ng], refs[ng : ng + nx - 1], refs[ng + nx - 1]
    group, dp = lax.axis_index("groups"), lax.axis_index("dp")
    core, x = lax.rem(dp, CORES), lax.div(dp, CORES)
    half, width, depth = send_ref.shape[1], own[0].shape[1], away[0].shape[1]
    copies = []

    def copy(ref, column, target):
        source = ref.at[:, pl.ds(pl.multiple_of(column, width), target.shape[1])]
        copies.append(pltpu.make_async_copy(source, target, sems.at[len(copies)]))
        copies[-1].start()

    copy(w_ref, (1 - core) * half, send_ref)
    for r in range(ng):
        copy(w_ref, core * half + lax.rem(group + r, ng) * width, own[r])
    for rel in range(1, nx):
        copy(x_ref, lax.rem(x + rel, nx) * depth, away[rel - 1])
    for each in copies:
        each.wait()


def pack_kernel(own_ref, swapped_ref, out_ref):
    _, width = own_ref.shape
    column = pl.multiple_of(lax.axis_index("groups") * width, width)
    out_ref[0] = own_ref[...]
    out_ref[1] = swapped_ref[:, pl.ds(column, width)]


def state_kernel(heads, ng, *refs):
    k_ref, v_ref, x_ref, gate_ref, forget_ref, reset_ref, xown_ref = refs[:7]
    chunks, sem = refs[7 : 7 + 3 * ng], refs[7 + 3 * ng]
    length = k_ref.shape[0]
    size, vsize = k_ref.shape[1] // heads, v_ref.shape[1] // heads
    group, dp = lax.axis_index("groups"), lax.axis_index("dp")
    depth = xown_ref.shape[1]
    column = pl.multiple_of(lax.div(dp, CORES) * depth, depth)
    copy = pltpu.make_async_copy(x_ref.at[:, pl.ds(column, depth)], xown_ref, sem)
    copy.start()
    count = lane_scan(padded(reset_ref[...].astype(f32)))[0:1]
    cumulative = lane_scan(padded(log_sigmoid(forget_ref[...])))[0:heads]
    total = cumulative[:, length - 1 : length]
    final = count[:, length - 1 : length]
    expo = jnp.where(count == final, total - cumulative + gate_ref[...], very_low)
    top = jnp.max(expo, axis=1, keepdims=True)
    weight = padded(jnp.exp(expo - top)).T
    gap = jnp.where(final > 0, very_low, total)
    for r in range(ng):
        own_ref, msg_ref, side_ref = chunks[3 * r : 3 * r + 3]
        for j in range(heads // ng):
            within = lax.rem(group + r, ng)
            head = j * ng + within

            def pick(values):
                chosen = values[j * ng]
                for i in range(1, ng):
                    chosen = jnp.where(within == i, values[j * ng + i], chosen)
                return chosen

            keys = k_ref[:, pl.ds(pl.multiple_of(head * size, size), size)].astype(f32)
            values = v_ref[:, pl.ds(pl.multiple_of(head * vsize, vsize), vsize)]
            scale = pick([weight[:, h : h + 1] for h in range(heads)])
            this_top = pick([top[h : h + 1] for h in range(heads)])
            this_gap = pick([gap[h : h + 1] for h in range(heads)])
            weighted = (keys * scale).astype(bf16)
            memory = lax.dot_general(
                weighted, values, (((0,), (0,)), ((), ())), preferred_element_type=f32
            )
            normer = jnp.sum(weighted.astype(f32), axis=0, keepdims=True)
            own_ref[j * size : (j + 1) * size, :] = memory
            side_ref[j * 8 : j * 8 + 1, :] = normer
            side_ref[j * 8 + 1 : j * 8 + 2, :] = jnp.broadcast_to(this_top, normer.shape)
            side_ref[j * 8 + 2 : j * 8 + 3, :] = jnp.broadcast_to(this_gap, normer.shape)
            store_message(msg_ref, j * (size + EXTRA), size, memory, normer, this_top)
    copy.wait()


def join(slots, prev_ref, own_ref, side_ref, out_ref):
    size = own_ref.shape[0] // slots
    stride = size + EXTRA
    for h in range(slots):
        memory, normer, top = load_message(prev_ref, h * stride, size)
        own_normer = side_ref[h * 8 : h * 8 + 1, :]
        own_top = side_ref[h * 8 + 1 : h * 8 + 2, 0:1]
        gap = side_ref[h * 8 + 2 : h * 8 + 3, 0:1]
        shifted = top + gap
        both = jnp.maximum(shifted, own_top)
        early = jnp.exp(shifted - both)
        late = jnp.exp(own_top - both)
        joined = early * memory.astype(f32) + late * own_ref[h * size : (h + 1) * size, :]
        normers = early * normer + late * own_normer
        store_message(out_ref, h * stride, size, joined, normers, both)


def combine_kernel(slots, sender, prev_ref, own_ref, side_ref, out_ref):
    place = lax.axis_index("ctx")

    @pl.when(place == sender)
    def _():
        join(slots, prev_ref, own_ref, side_ref, out_ref)

    @pl.when(place != sender)
    def _():
        out_ref[...] = prev_ref[...]


def mix_kernel(message_ref, piece_ref, out_ref):
    place = lax.axis_index("ctx")
    rows = piece_ref.shape[1]

    @pl.when(place == 0)
    def _():
        out_ref[...] = message_ref[...]

    @pl.when(place != 0)
    def _():
        for j in range(CORES):
            out_ref[j * rows : (j + 1) * rows, :] = piece_ref[j]
        rest = out_ref.shape[0] - CORES * rows
        out_ref[CORES * rows :, :] = jnp.zeros((rest, out_ref.shape[1]), out_ref.dtype)


def pick_kernel(inner_ref, outer_ref, out_ref):
    place = lax.axis_index("ctx")
    rows = out_ref.shape[1]
    inner = jnp.logical_or(place == 1, place == 2)

    @pl.when(inner)
    def _():
        out_ref[...] = inner_ref[...]

    @pl.when(jnp.logical_not(inner))
    def _():
        for j in range(CORES):
            out_ref[j] = outer_ref[j * rows : (j + 1) * rows, :]


def away_kernel(nz, ng, phase, swapped, count, *refs):
    first = 2 if phase else 1
    tokens, parts = refs[:count], refs[count : count + first + nz - 1]
    outs, whole = refs[count + len(parts) : -1], refs[-1]
    rows, width = parts[-1].shape[1:]
    place, group = lax.axis_index("ctx"), lax.axis_index("groups")
    core = lax.rem(lax.axis_index("dp"), CORES)
    if phase:
        column = pl.multiple_of(lax.rem(group + phase, ng) * width, width)
        values = [(parts[0][...], parts[1][:, pl.ds(column, width)])]
    else:
        values = [(parts[0][0], parts[0][1])]
    for part in parts[first:]:
        values.append((part[0], part[1]))
    for s in range(nz):
        source = place ^ s
        if swapped and s >= 2:
            inner = jnp.logical_or(place == 1, place == 2)
            source = jnp.where(inner, place ^ (5 - s), source)
        for j in range(CORES):
            owner = lax.rem(core + j, CORES)
            row = pl.multiple_of((owner * nz + source) * rows, rows)
            whole[pl.ds(row, rows), :] = values[s][j]
    for token, out in zip(tokens, outs):
        value = jnp.dot(token[...], whole[...], preferred_element_type=f32)
        out[...] = value.astype(out.dtype)


def keep_kernel(*refs):
    tokens, whole, outs = refs[:CORES], refs[CORES], refs[CORES + 1 :]
    for token, out in zip(tokens, outs):
        out[...] = jnp.dot(token[...], whole[...], preferred_element_type=f32)


def read_kernel(heads, ng, nx, hops, phase, *refs):
    partials = [refs[j * nx : (j + 1) * nx] for j in range(CORES)]
    k_ref, v_ref, gate_ref, forget_ref, reset_ref = refs[CORES * nx : CORES * nx + 5]
    at = CORES * nx + 5
    done = phase if phase == ng - 1 else 0
    states, earlier = refs[at : at + hops], refs[at + hops : at + hops + done]
    out_ref, state, sem = refs[at + hops + done :]
    length = k_ref.shape[0]
    size, vsize = k_ref.shape[1] // heads, v_ref.shape[1] // heads
    factor = size ** (-0.5)
    stride = size + EXTRA
    group, dp, place = (lax.axis_index(a) for a in AXES)
    core = lax.rem(dp, CORES)

    def slot_of(j):
        return lax.rem(core + j, CORES)

    def head_of(j, r):
        return slot_of(j) * ng + lax.rem(group + r, ng)

    for h in range(hops):

        @pl.when(place == h + 1)
        def _():
            pltpu.make_async_copy(states[h], state, sem).start()

    @pl.when(place == 0)
    def _():
        state[...] = jnp.zeros_like(state)

    t_at = lax.broadcasted_iota(jnp.int32, (length, length), 0)
    s_at = lax.broadcasted_iota(jnp.int32, (length, length), 1)
    forget = [log_sigmoid(forget_ref[pl.ds(head_of(j, phase), 1), :]) for j in range(CORES)]
    running = lane_scan(padded(jnp.concatenate([reset_ref[...].astype(f32)] + forget, axis=0)))
    running_rows = running.T
    count, count_rows = running[0:1], running_rows[:, 0:1]
    linked = jnp.logical_and(count_rows == count, t_at >= s_at)
    exponents = []
    for j in range(CORES):
        exponents.append(
            jnp.where(
                linked,
                running_rows[:, 1 + j : 2 + j]
                - running[1 + j : 2 + j]
                + gate_ref[pl.ds(head_of(j, phase), 1), :],
                very_low,
            )
        )

    @pl.when(place > 0)
    def _():
        pltpu.make_async_copy(states[0], state, sem).wait()

    for j in range(CORES):
        total = partials[j][0][...]
        for other in partials[j][1:]:
            total = total + other[...].astype(f32)
        query = total.astype(bf16)
        head = head_of(j, phase)
        keys = k_ref[:, pl.ds(pl.multiple_of(head * size, size), size)]
        values = v_ref[:, pl.ds(pl.multiple_of(head * vsize, vsize), vsize)]
        base = pl.multiple_of(slot_of(j) * stride, EXTRA)
        memory = state[pl.ds(base, size), :]
        extra = state[pl.ds(pl.multiple_of(base + size, EXTRA), EXTRA), :].astype(f32)
        normer = (extra[0:1] + extra[1:2] + extra[2:3]).astype(bf16).astype(f32)
        top = extra[3:4, 0:1] + extra[4:5, 0:1] + extra[5:6, 0:1]
        top = jnp.where(place == 0, very_low, top)
        exponent = exponents[j]
        carried = jnp.where(count_rows == 0.0, running_rows[:, 1 + j : 2 + j] + top, very_low)
        row_max = jnp.maximum(jnp.max(exponent, axis=1, keepdims=True), carried)
        scores = lax.dot_general(
            query, keys, (((1,), (1,)), ((), ())), preferred_element_type=f32
        )
        weighted = (jnp.exp(exponent - row_max) * (scores * factor)).astype(bf16)
        scale = jnp.exp(carried - row_max) * factor
        cross = jnp.dot(query, memory, preferred_element_type=f32)
        inter = jnp.sum(query.astype(f32) * normer, axis=1, keepdims=True)
        numerator = jnp.dot(weighted, values, preferred_element_type=f32) + scale * cross
        denominator = jnp.sum(weighted.astype(f32), axis=1, keepdims=True) + scale * inter
        floor = jnp.exp(jnp.maximum(-row_max, 0.0))
        hidden = (numerator / jnp.maximum(jnp.abs(denominator), floor)).astype(bf16)
        if phase < ng - 1:
            out_ref[:, j * vsize : (j + 1) * vsize] = hidden
        else:
            target = pl.multiple_of(head_of(j, phase) * vsize, vsize)
            out_ref[:, pl.ds(target, vsize)] = hidden
    if phase == ng - 1:
        for r in range(phase):
            for j in range(CORES):
                target = pl.multiple_of(head_of(j, r) * vsize, vsize)
                out_ref[:, pl.ds(target, vsize)] = earlier[r][:, j * vsize : (j + 1) * vsize]


VMEM = pl.BlockSpec(memory_space=pltpu.VMEM)
ANY = pl.BlockSpec(memory_space=pl.ANY)


def links(z):
    return {z: z + 1, z + 1: z}


def compact(mesh):
    return mesh.shape["ctx"] == 4 and mesh.shape["groups"] == CORES == 2


def make_body(mesh):
    ng, nd, nz = (mesh.shape[a] for a in AXES)
    nx = nd // CORES

    def send(value, where):
        return lax.ppermute(value, AXES, moves(mesh, where))

    def over_core(value):
        return send(value, lambda g, x, k, z: (g, x, 1 - k, z))

    def call(kernel, *args, **options):
        params = pltpu.CompilerParams(vmem_limit_bytes=20 * 2**20)
        return pl.pallas_call(kernel, compiler_params=params, **options)(*args)

    def body(normed_input, query_weight, key_vectors, value_vectors, input_gate, forget_gate, resets):
        _, length, features = normed_input.shape
        heads = input_gate.shape[1]
        columns = query_weight.shape[1]
        width = columns // (ng * CORES)
        size = columns // heads
        keys, values = key_vectors[0], value_vectors[0]
        gate, forget = input_gate[0], forget_gate[0]
        vwidth = values.shape[1]
        half = columns // CORES
        depth = features // nx
        flat = normed_input[0]

        stride = size + EXTRA
        vsize = vwidth // heads
        slots = heads // ng
        message = jax.ShapeDtypeStruct((slots * stride, vsize), bf16)
        block = jax.ShapeDtypeStruct((length, depth), flat.dtype)
        hbm_tokens = pltpu.with_memory_space_constraint(flat, pltpu.HBM)
        hbm_weight = pltpu.with_memory_space_constraint(query_weight, pltpu.HBM)
        rows = query_weight.shape[0]
        quarter = jax.ShapeDtypeStruct((rows, width), query_weight.dtype)
        sliced = call(
            functools.partial(slice_kernel, ng, nx),
            hbm_tokens, hbm_weight,
            out_shape=(
                jax.ShapeDtypeStruct((rows, half), query_weight.dtype),
                *[quarter] * ng,
                *[block] * (nx - 1),
            ),
            in_specs=[ANY] * 2,
            out_specs=(VMEM,) * (ng + nx),
            scratch_shapes=[pltpu.SemaphoreType.DMA((ng + nx,))],
        )
        swapped = over_core(sliced[0])
        own_parts = sliced[1 : 1 + ng]
        arrived = [
            send(sliced[ng + rel], lambda g, x, k, z: (g, (x + rel) % nx, k, z))
            for rel in range(1, nx)
        ]
        packed = call(
            pack_kernel,
            own_parts[0], swapped,
            out_shape=jax.ShapeDtypeStruct((CORES, rows, width), bf16),
            in_specs=[VMEM] * 2,
            out_specs=VMEM,
        )
        prepared = call(
            functools.partial(state_kernel, heads, ng),
            keys, values, hbm_tokens, gate, forget, resets,
            out_shape=(
                block,
                *[
                    jax.ShapeDtypeStruct((slots * size, vsize), f32),
                    message,
                    jax.ShapeDtypeStruct((slots * 8, vsize), f32),
                ]
                * ng,
            ),
            in_specs=[VMEM] * 2 + [ANY] + [VMEM] * 3,
            out_specs=(VMEM,) * (1 + 3 * ng),
            scratch_shapes=[pltpu.SemaphoreType.DMA(())],
        )
        tokens = [prepared[0]]
        tokens.append(over_core(tokens[0]))
        for rel, value in enumerate(arrived):
            tokens.extend([value, over_core(value)])
        pieces = [[packed]] + [[own_parts[r], swapped] for r in range(1, ng)]

        def over_ctx(value, targets):
            return send(
                value,
                lambda g, x, k, z: (g, x, k, targets[z]) if z in targets else (g, x, 1 - k, z),
            )

        own = [prepared[1 + 3 * r] for r in range(ng)]
        first = [prepared[2 + 3 * r] for r in range(ng)]
        side = [prepared[3 + 3 * r] for r in range(ng)]
        states = [[] for _ in range(ng)]

        def extend(hop, r):
            message_out = call(
                functools.partial(combine_kernel, slots, hop - 1),
                states[r][-1], own[r], side[r],
                out_shape=message,
                in_specs=[VMEM] * 3,
                out_specs=VMEM,
            )
            states[r].append(over_ctx(message_out, links(hop - 1)))

        if compact(mesh):
            near = over_ctx(packed, {z: z ^ 1 for z in range(nz)})
            middle = over_ctx(packed, links(1))
            across = over_ctx(near, links(1))
            gathered = {1: near}
            for r, inside in enumerate((middle, across)):
                mixed = call(
                    mix_kernel,
                    first[r], inside,
                    out_shape=message,
                    in_specs=[VMEM] * 2,
                    out_specs=VMEM,
                )
                outside = over_ctx(mixed, {**links(0), **links(2)})
                states[r].append(outside)
                gathered[r + 2] = call(
                    pick_kernel,
                    inside, outside,
                    out_shape=jax.ShapeDtypeStruct(packed.shape, bf16),
                    in_specs=[VMEM] * 2,
                    out_specs=VMEM,
                )
        else:
            gathered = {s: over_ctx(packed, {z: z ^ s for z in range(nz)}) for s in range(1, nz)}
            for r in range(ng):
                states[r].append(over_ctx(first[r], links(0)))
        for hop in range(2, nz):
            for r in range(ng):
                extend(hop, r)
        for s in range(1, nz):
            pieces[0].append(gathered[s])
            for r in range(1, ng):
                pieces[r].append(send(gathered[s], lambda g, x, k, z: ((g - r) % ng, x, k, z)))
        results = []
        for r in range(ng):
            piece = jax.ShapeDtypeStruct((length, width), f32)
            small = jax.ShapeDtypeStruct((length, width), bf16)
            count = CORES * (nx - 1)
            sent = call(
                functools.partial(away_kernel, nz, ng, r, compact(mesh), count),
                *tokens[CORES:], *pieces[r],
                out_shape=(small,) * count + (jax.ShapeDtypeStruct((depth, width), bf16),),
                in_specs=[VMEM] * (count + len(pieces[r])),
                out_specs=(VMEM,) * (count + 1),
            )
            kept = call(
                keep_kernel,
                *tokens[:CORES], sent[-1],
                out_shape=(piece,) * CORES,
                in_specs=[VMEM] * (CORES + 1),
                out_specs=(VMEM,) * CORES,
            )
            sums = [*kept, *sent[:-1]]
            partials = [[sums[0]], [over_core(sums[1])]]
            for rel in range(1, nx):
                for j in range(CORES):
                    partials[j].append(
                        send(
                            sums[CORES * rel + j], lambda g, x, k, z: (g, (x - rel) % nx, k ^ j, z)
                        )
                    )
            last = r == ng - 1
            results.append(
                call(
                    functools.partial(read_kernel, heads, ng, nx, nz - 1, r),
                    *partials[0], *partials[1], keys, values, gate, forget, resets,
                    *states[r], *(results if last else []),
                    out_shape=jax.ShapeDtypeStruct(
                        (length, vwidth if last else CORES * vsize), bf16
                    ),
                    in_specs=[VMEM] * (CORES * nx + 5)
                    + [ANY] * (nz - 1) + [VMEM] * (r if last else 0),
                    out_specs=VMEM,
                    scratch_shapes=[
                        pltpu.VMEM(message.shape, bf16),
                        pltpu.SemaphoreType.DMA(()),
                    ],
                )
            )
        hidden = results[-1]
        return hidden[None]

    return body


def solution(mesh):
    return jax.shard_map(
        make_body(mesh),
        mesh=mesh,
        in_specs=(
            P(("groups", "dp"), "ctx", None),
            P(("dp", "ctx"), None),
            P(("groups", "dp"), "ctx", None),
            P(("groups", "dp"), "ctx", None),
            P(("groups", "dp"), None, "ctx"),
            P(("groups", "dp"), None, "ctx"),
            P(("groups", "dp"), "ctx"),
        ),
        out_specs=P(("groups", "dp"), "ctx", None),
        check_vma=False,
    )
```

```python
import functools

import jax
import jax.numpy as jnp
from jax import lax
from jax.experimental import pallas as pl
from jax.experimental.pallas import tpu as pltpu
from jax.sharding import PartitionSpec as P


very_low = -1e30
AXES = ("groups", "dp", "ctx")
CORES = 2
EXTRA = 16
f32 = jnp.float32
bf16 = jnp.bfloat16


def moves(mesh, where):
    ng, nd, nz = (mesh.shape[a] for a in AXES)
    pairs = []
    for g in range(ng):
        for x in range(nd // CORES):
            for k in range(CORES):
                for z in range(nz):
                    to = where(g, x, k, z)
                    if to is not None:
                        g2, x2, k2, z2 = to
                        source = (g * nd + x * CORES + k) * nz + z
                        pairs.append((source, (g2 * nd + x2 * CORES + k2) * nz + z2))
    return pairs


def lane_scan(values):
    length = values.shape[1]
    lane = lax.broadcasted_iota(jnp.int32, values.shape, 1)
    step = 1
    while step < length:
        moved = pltpu.roll(values, step, 1)
        values = values + jnp.where(lane >= step, moved, jnp.zeros_like(values))
        step *= 2
    return values


def log_sigmoid(x):
    return jnp.minimum(x, 0.0) - jnp.log1p(jnp.exp(-jnp.abs(x)))


def padded(values):
    rows = values.shape[0]
    if rows % 8 == 0:
        return values
    fill = jnp.zeros((8 - rows % 8, values.shape[1]), values.dtype)
    return jnp.concatenate([values, fill], axis=0)


def split_rows(value):
    high = value.astype(bf16)
    rest = value - high.astype(f32)
    mid = rest.astype(bf16)
    low = (rest - mid.astype(f32)).astype(bf16)
    return high, mid, low


def store_message(out_ref, base, size, memory, normer, top):
    out_ref[base : base + size, :] = memory.astype(bf16)
    n_parts = split_rows(normer)
    t_parts = split_rows(jnp.broadcast_to(top, normer.shape))
    row = lax.broadcasted_iota(jnp.int32, (EXTRA, normer.shape[1]), 0)
    block = jnp.zeros((EXTRA, normer.shape[1]), f32)
    for i, part in enumerate(n_parts + t_parts):
        block = jnp.where(row == i, part.astype(f32), block)
    out_ref[base + size : base + size + EXTRA, :] = block.astype(bf16)


def load_message(ref, base, size):
    extra = ref[base + size : base + size + EXTRA, :].astype(f32)
    normer = extra[0:1] + extra[1:2] + extra[2:3]
    top = extra[3:4, 0:1] + extra[4:5, 0:1] + extra[5:6, 0:1]
    return ref[base : base + size, :], normer, top


def slice_kernel(ng, nx, x_ref, w_ref, send_ref, *refs):
    own, away, sems = refs[:ng], refs[ng : ng + nx - 1], refs[ng + nx - 1]
    group, dp = lax.axis_index("groups"), lax.axis_index("dp")
    core, x = lax.rem(dp, CORES), lax.div(dp, CORES)
    half, width, depth = send_ref.shape[1], own[0].shape[1], away[0].shape[1]
    copies = []

    def copy(ref, column, target):
        source = ref.at[:, pl.ds(pl.multiple_of(column, width), target.shape[1])]
        copies.append(pltpu.make_async_copy(source, target, sems.at[len(copies)]))
        copies[-1].start()

    copy(w_ref, (1 - core) * half, send_ref)
    for r in range(ng):
        copy(w_ref, core * half + lax.rem(group + r, ng) * width, own[r])
    for rel in range(1, nx):
        copy(x_ref, lax.rem(x + rel, nx) * depth, away[rel - 1])
    for each in copies:
        each.wait()


def pack_kernel(own_ref, swapped_ref, out_ref):
    _, width = own_ref.shape
    column = pl.multiple_of(lax.axis_index("groups") * width, width)
    out_ref[0] = own_ref[...]
    out_ref[1] = swapped_ref[:, pl.ds(column, width)]


def state_kernel(heads, ng, *refs):
    k_ref, v_ref, x_ref, gate_ref, forget_ref, reset_ref, xown_ref = refs[:7]
    chunks, sem = refs[7 : 7 + 3 * ng], refs[7 + 3 * ng]
    length = k_ref.shape[0]
    size, vsize = k_ref.shape[1] // heads, v_ref.shape[1] // heads
    group, dp = lax.axis_index("groups"), lax.axis_index("dp")
    depth = xown_ref.shape[1]
    column = pl.multiple_of(lax.div(dp, CORES) * depth, depth)
    copy = pltpu.make_async_copy(x_ref.at[:, pl.ds(column, depth)], xown_ref, sem)
    copy.start()
    count = lane_scan(padded(reset_ref[...].astype(f32)))[0:1]
    cumulative = lane_scan(padded(log_sigmoid(forget_ref[...])))[0:heads]
    total = cumulative[:, length - 1 : length]
    final = count[:, length - 1 : length]
    expo = jnp.where(count == final, total - cumulative + gate_ref[...], very_low)
    top = jnp.max(expo, axis=1, keepdims=True)
    weight = padded(jnp.exp(expo - top)).T
    gap = jnp.where(final > 0, very_low, total)
    for r in range(ng):
        own_ref, msg_ref, side_ref = chunks[3 * r : 3 * r + 3]
        for j in range(heads // ng):
            within = lax.rem(group + r, ng)
            head = j * ng + within

            def pick(values):
                chosen = values[j * ng]
                for i in range(1, ng):
                    chosen = jnp.where(within == i, values[j * ng + i], chosen)
                return chosen

            keys = k_ref[:, pl.ds(pl.multiple_of(head * size, size), size)].astype(f32)
            values = v_ref[:, pl.ds(pl.multiple_of(head * vsize, vsize), vsize)]
            scale = pick([weight[:, h : h + 1] for h in range(heads)])
            this_top = pick([top[h : h + 1] for h in range(heads)])
            this_gap = pick([gap[h : h + 1] for h in range(heads)])
            weighted = (keys * scale).astype(bf16)
            memory = lax.dot_general(
                weighted, values, (((0,), (0,)), ((), ())), preferred_element_type=f32
            )
            normer = jnp.sum(weighted.astype(f32), axis=0, keepdims=True)
            own_ref[j * size : (j + 1) * size, :] = memory
            side_ref[j * 8 : j * 8 + 1, :] = normer
            side_ref[j * 8 + 1 : j * 8 + 2, :] = jnp.broadcast_to(this_top, normer.shape)
            side_ref[j * 8 + 2 : j * 8 + 3, :] = jnp.broadcast_to(this_gap, normer.shape)
            store_message(msg_ref, j * (size + EXTRA), size, memory, normer, this_top)
    copy.wait()


def join(slots, prev_ref, own_ref, side_ref, out_ref):
    size = own_ref.shape[0] // slots
    stride = size + EXTRA
    for h in range(slots):
        memory, normer, top = load_message(prev_ref, h * stride, size)
        own_normer = side_ref[h * 8 : h * 8 + 1, :]
        own_top = side_ref[h * 8 + 1 : h * 8 + 2, 0:1]
        gap = side_ref[h * 8 + 2 : h * 8 + 3, 0:1]
        shifted = top + gap
        both = jnp.maximum(shifted, own_top)
        early = jnp.exp(shifted - both)
        late = jnp.exp(own_top - both)
        joined = early * memory.astype(f32) + late * own_ref[h * size : (h + 1) * size, :]
        normers = early * normer + late * own_normer
        store_message(out_ref, h * stride, size, joined, normers, both)


def combine_kernel(slots, sender, prev_ref, own_ref, side_ref, out_ref):
    place = lax.axis_index("ctx")

    @pl.when(place == sender)
    def _():
        join(slots, prev_ref, own_ref, side_ref, out_ref)

    @pl.when(place != sender)
    def _():
        out_ref[...] = prev_ref[...]


def mix_kernel(message_ref, piece_ref, out_ref):
    place = lax.axis_index("ctx")
    rows = piece_ref.shape[1]

    @pl.when(place == 0)
    def _():
        out_ref[...] = message_ref[...]

    @pl.when(place != 0)
    def _():
        for j in range(CORES):
            out_ref[j * rows : (j + 1) * rows, :] = piece_ref[j]
        rest = out_ref.shape[0] - CORES * rows
        out_ref[CORES * rows :, :] = jnp.zeros((rest, out_ref.shape[1]), out_ref.dtype)


def pick_kernel(inner_ref, outer_ref, out_ref):
    place = lax.axis_index("ctx")
    rows = out_ref.shape[1]
    inner = jnp.logical_or(place == 1, place == 2)

    @pl.when(inner)
    def _():
        out_ref[...] = inner_ref[...]

    @pl.when(jnp.logical_not(inner))
    def _():
        for j in range(CORES):
            out_ref[j] = outer_ref[j * rows : (j + 1) * rows, :]


def away_kernel(nz, ng, phase, swapped, count, *refs):
    first = 2 if phase else 1
    tokens, parts = refs[:count], refs[count : count + first + nz - 1]
    outs, whole = refs[count + len(parts) : -1], refs[-1]
    rows, width = parts[-1].shape[1:]
    place, group = lax.axis_index("ctx"), lax.axis_index("groups")
    core = lax.rem(lax.axis_index("dp"), CORES)
    if phase:
        column = pl.multiple_of(lax.rem(group + phase, ng) * width, width)
        values = [(parts[0][...], parts[1][:, pl.ds(column, width)])]
    else:
        values = [(parts[0][0], parts[0][1])]
    for part in parts[first:]:
        values.append((part[0], part[1]))
    for s in range(nz):
        source = place ^ s
        if swapped and s >= 2:
            inner = jnp.logical_or(place == 1, place == 2)
            source = jnp.where(inner, place ^ (5 - s), source)
        for j in range(CORES):
            owner = lax.rem(core + j, CORES)
            row = pl.multiple_of((owner * nz + source) * rows, rows)
            whole[pl.ds(row, rows), :] = values[s][j]
    for token, out in zip(tokens, outs):
        value = jnp.dot(token[...], whole[...], preferred_element_type=f32)
        out[...] = value.astype(out.dtype)


def keep_kernel(*refs):
    tokens, whole, outs = refs[:CORES], refs[CORES], refs[CORES + 1 :]
    for token, out in zip(tokens, outs):
        out[...] = jnp.dot(token[...], whole[...], preferred_element_type=f32)


def head_of(j, r, ng):
    slot = lax.rem(lax.rem(lax.axis_index("dp"), CORES) + j, CORES)
    return slot * ng + lax.rem(lax.axis_index("groups") + r, ng)


def decay_kernel(ng, gate_ref, forget_ref, reset_ref, *outs):
    length = reset_ref.shape[1]
    t_at = lax.broadcasted_iota(jnp.int32, (length, length), 0)
    s_at = lax.broadcasted_iota(jnp.int32, (length, length), 1)
    pairs = [(j, r) for r in range(ng) for j in range(CORES)]
    forget = [log_sigmoid(forget_ref[pl.ds(head_of(j, r, ng), 1), :]) for j, r in pairs]
    running = lane_scan(padded(jnp.concatenate([reset_ref[...].astype(f32)] + forget, axis=0)))
    running_rows = running.T
    count, count_rows = running[0:1], running_rows[:, 0:1]
    linked = jnp.logical_and(count_rows == count, t_at >= s_at)
    for at, (j, r) in enumerate(pairs):
        decay_ref, column_ref = outs[2 * r], outs[2 * r + 1]
        cum_t = running_rows[:, 1 + at : 2 + at]
        exponent = jnp.where(
            linked,
            cum_t - running[1 + at : 2 + at] + gate_ref[pl.ds(head_of(j, r, ng), 1), :],
            very_low,
        )
        top = jnp.max(exponent, axis=1, keepdims=True)
        decay_ref[j] = jnp.exp(exponent - top)
        lane = lax.broadcasted_iota(jnp.int32, (length, 128), 1)
        columns = jnp.where(lane == 0, top, jnp.where(lane == 1, cum_t, count_rows))
        column_ref[j] = columns


def read_kernel(heads, ng, nx, hops, phase, *refs):
    partials = [refs[j * nx : (j + 1) * nx] for j in range(CORES)]
    k_ref, v_ref, decay_ref, column_ref = refs[CORES * nx : CORES * nx + 4]
    at = CORES * nx + 4
    states = refs[at : at + hops]
    out_ref, state, result, sem, out_sems = refs[at + hops + (1 if phase else 0) :]
    size, vsize = k_ref.shape[1] // heads, v_ref.shape[1] // heads
    factor = size ** (-0.5)
    stride = size + EXTRA
    place = lax.axis_index("ctx")
    core = lax.rem(lax.axis_index("dp"), CORES)
    for h in range(hops):

        @pl.when(place == h + 1)
        def _():
            pltpu.make_async_copy(states[h], state, sem).start()

    @pl.when(place == 0)
    def _():
        state[...] = jnp.zeros_like(state)

    queries, scores = [], []
    for j in range(CORES):
        head = head_of(j, phase, ng)
        total = partials[j][0][...]
        for other in partials[j][1:]:
            total = total + other[...].astype(f32)
        query = total.astype(bf16)
        keys = k_ref[:, pl.ds(pl.multiple_of(head * size, size), size)]
        queries.append(query)
        scores.append(
            lax.dot_general(query, keys, (((1,), (1,)), ((), ())), preferred_element_type=f32)
        )

    @pl.when(place > 0)
    def _():
        pltpu.make_async_copy(states[0], state, sem).wait()

    copies = []
    for j in range(CORES):
        head = head_of(j, phase, ng)
        query = queries[j]
        column = pl.multiple_of(head * vsize, vsize)
        values = v_ref[:, pl.ds(column, vsize)]
        base = pl.multiple_of(lax.rem(core + j, CORES) * stride, EXTRA)
        memory = state[pl.ds(base, size), :]
        extra = state[pl.ds(pl.multiple_of(base + size, EXTRA), EXTRA), :].astype(f32)
        normer = (extra[0:1] + extra[1:2] + extra[2:3]).astype(bf16).astype(f32)
        top = extra[3:4, 0:1] + extra[4:5, 0:1] + extra[5:6, 0:1]
        top = jnp.where(place == 0, very_low, top)
        columns = column_ref[j]
        block_max, cum_t, count_rows = columns[:, 0:1], columns[:, 1:2], columns[:, 2:3]
        carried = jnp.where(count_rows == 0.0, cum_t + top, very_low)
        row_max = jnp.maximum(block_max, carried)
        weighted = (decay_ref[j] * (scores[j] * factor)).astype(bf16)
        within = jnp.exp(block_max - row_max)
        scale = jnp.exp(carried - row_max) * factor
        cross = jnp.dot(query, memory, preferred_element_type=f32)
        inter = jnp.sum(query.astype(f32) * normer, axis=1, keepdims=True)
        numerator = (
            within * jnp.dot(weighted, values, preferred_element_type=f32) + scale * cross
        )
        denominator = (
            within * jnp.sum(weighted.astype(f32), axis=1, keepdims=True) + scale * inter
        )
        floor = jnp.exp(jnp.maximum(-row_max, 0.0))
        result[j] = (numerator / jnp.maximum(jnp.abs(denominator), floor)).astype(bf16)
        copy = pltpu.make_async_copy(
            result.at[j], out_ref.at[:, pl.ds(column, vsize)], out_sems.at[j]
        )
        copy.start()
        copies.append(copy)
    for copy in copies:
        copy.wait()


VMEM = pl.BlockSpec(memory_space=pltpu.VMEM)
ANY = pl.BlockSpec(memory_space=pl.ANY)


def links(z):
    return {z: z + 1, z + 1: z}


def compact(mesh):
    return mesh.shape["ctx"] == 4 and mesh.shape["groups"] == CORES == 2


def make_body(mesh):
    ng, nd, nz = (mesh.shape[a] for a in AXES)
    nx = nd // CORES

    def send(value, where):
        return lax.ppermute(value, AXES, moves(mesh, where))

    def over_core(value):
        return send(value, lambda g, x, k, z: (g, x, 1 - k, z))

    def call(kernel, *args, **options):
        params = pltpu.CompilerParams(vmem_limit_bytes=20 * 2**20)
        return pl.pallas_call(kernel, compiler_params=params, **options)(*args)

    def body(normed_input, query_weight, key_vectors, value_vectors, input_gate, forget_gate, resets):
        _, length, features = normed_input.shape
        heads = input_gate.shape[1]
        columns = query_weight.shape[1]
        width = columns // (ng * CORES)
        size = columns // heads
        keys, values = key_vectors[0], value_vectors[0]
        gate, forget = input_gate[0], forget_gate[0]
        vwidth = values.shape[1]
        half = columns // CORES
        depth = features // nx
        flat = normed_input[0]

        stride = size + EXTRA
        vsize = vwidth // heads
        slots = heads // ng
        message = jax.ShapeDtypeStruct((slots * stride, vsize), bf16)
        block = jax.ShapeDtypeStruct((length, depth), flat.dtype)
        hbm_tokens = pltpu.with_memory_space_constraint(flat, pltpu.HBM)
        hbm_weight = pltpu.with_memory_space_constraint(query_weight, pltpu.HBM)
        rows = query_weight.shape[0]
        quarter = jax.ShapeDtypeStruct((rows, width), query_weight.dtype)
        sliced = call(
            functools.partial(slice_kernel, ng, nx),
            hbm_tokens, hbm_weight,
            out_shape=(
                jax.ShapeDtypeStruct((rows, half), query_weight.dtype),
                *[quarter] * ng,
                *[block] * (nx - 1),
            ),
            in_specs=[ANY] * 2,
            out_specs=(VMEM,) * (ng + nx),
            scratch_shapes=[pltpu.SemaphoreType.DMA((ng + nx,))],
        )
        swapped = over_core(sliced[0])
        own_parts = sliced[1 : 1 + ng]
        arrived = [
            send(sliced[ng + rel], lambda g, x, k, z: (g, (x + rel) % nx, k, z))
            for rel in range(1, nx)
        ]
        packed = call(
            pack_kernel,
            own_parts[0], swapped,
            out_shape=jax.ShapeDtypeStruct((CORES, rows, width), bf16),
            in_specs=[VMEM] * 2,
            out_specs=VMEM,
        )
        prepared = call(
            functools.partial(state_kernel, heads, ng),
            keys, values, hbm_tokens, gate, forget, resets,
            out_shape=(
                block,
                *[
                    jax.ShapeDtypeStruct((slots * size, vsize), f32),
                    message,
                    jax.ShapeDtypeStruct((slots * 8, vsize), f32),
                ]
                * ng,
            ),
            in_specs=[VMEM] * 2 + [ANY] + [VMEM] * 3,
            out_specs=(VMEM,) * (1 + 3 * ng),
            scratch_shapes=[pltpu.SemaphoreType.DMA(())],
        )
        tokens = [prepared[0]]
        tokens.append(over_core(tokens[0]))
        for rel, value in enumerate(arrived):
            tokens.extend([value, over_core(value)])
        pieces = [[packed]] + [[own_parts[r], swapped] for r in range(1, ng)]

        def over_ctx(value, targets):
            return send(
                value,
                lambda g, x, k, z: (g, x, k, targets[z]) if z in targets else (g, x, 1 - k, z),
            )

        own = [prepared[1 + 3 * r] for r in range(ng)]
        first = [prepared[2 + 3 * r] for r in range(ng)]
        side = [prepared[3 + 3 * r] for r in range(ng)]
        states = [[] for _ in range(ng)]

        def extend(hop, r):
            message_out = call(
                functools.partial(combine_kernel, slots, hop - 1),
                states[r][-1], own[r], side[r],
                out_shape=message,
                in_specs=[VMEM] * 3,
                out_specs=VMEM,
            )
            states[r].append(over_ctx(message_out, links(hop - 1)))

        if compact(mesh):
            near = over_ctx(packed, {z: z ^ 1 for z in range(nz)})
            middle = over_ctx(packed, links(1))
            across = over_ctx(near, links(1))
            gathered = {1: near}
            for r, inside in enumerate((middle, across)):
                mixed = call(
                    mix_kernel,
                    first[r], inside,
                    out_shape=message,
                    in_specs=[VMEM] * 2,
                    out_specs=VMEM,
                )
                outside = over_ctx(mixed, {**links(0), **links(2)})
                states[r].append(outside)
                gathered[r + 2] = call(
                    pick_kernel,
                    inside, outside,
                    out_shape=jax.ShapeDtypeStruct(packed.shape, bf16),
                    in_specs=[VMEM] * 2,
                    out_specs=VMEM,
                )
        else:
            gathered = {s: over_ctx(packed, {z: z ^ s for z in range(nz)}) for s in range(1, nz)}
            for r in range(ng):
                states[r].append(over_ctx(first[r], links(0)))
        for hop in range(2, nz):
            for r in range(ng):
                extend(hop, r)
        for s in range(1, nz):
            pieces[0].append(gathered[s])
            for r in range(1, ng):
                pieces[r].append(send(gathered[s], lambda g, x, k, z: ((g - r) % ng, x, k, z)))
        decays = call(
            functools.partial(decay_kernel, ng),
            gate, forget, resets,
            out_shape=(
                jax.ShapeDtypeStruct((CORES, length, length), f32),
                jax.ShapeDtypeStruct((CORES, length, 128), f32),
            )
            * ng,
            in_specs=[VMEM] * 3,
            out_specs=(VMEM,) * (2 * ng),
        )
        hidden = None
        for r in range(ng):
            piece = jax.ShapeDtypeStruct((length, width), f32)
            small = jax.ShapeDtypeStruct((length, width), bf16)
            count = CORES * (nx - 1)
            sent = call(
                functools.partial(away_kernel, nz, ng, r, compact(mesh), count),
                *tokens[CORES:], *pieces[r],
                out_shape=(small,) * count + (jax.ShapeDtypeStruct((depth, width), bf16),),
                in_specs=[VMEM] * (count + len(pieces[r])),
                out_specs=(VMEM,) * (count + 1),
            )
            kept = call(
                keep_kernel,
                *tokens[:CORES], sent[-1],
                out_shape=(piece,) * CORES,
                in_specs=[VMEM] * (CORES + 1),
                out_specs=(VMEM,) * CORES,
            )
            sums = [*kept, *sent[:-1]]
            partials = [[sums[0]], [over_core(sums[1])]]
            for rel in range(1, nx):
                for j in range(CORES):
                    partials[j].append(
                        send(
                            sums[CORES * rel + j], lambda g, x, k, z: (g, (x - rel) % nx, k ^ j, z)
                        )
                    )
            count = CORES * nx + 4 + nz - 1
            hidden = call(
                functools.partial(read_kernel, heads, ng, nx, nz - 1, r),
                *partials[0], *partials[1], keys, values, *decays[2 * r : 2 * r + 2],
                *states[r], *([hidden] if r else []),
                out_shape=jax.ShapeDtypeStruct((length, vwidth), bf16),
                in_specs=[VMEM] * (CORES * nx + 4) + [ANY] * (nz - 1 + (1 if r else 0)),
                out_specs=ANY,
                input_output_aliases={count: 0} if r else {},
                scratch_shapes=[
                    pltpu.VMEM(message.shape, bf16),
                    pltpu.VMEM((CORES, length, vsize), bf16),
                    pltpu.SemaphoreType.DMA(()),
                    pltpu.SemaphoreType.DMA((CORES,)),
                ],
            )
        return hidden[None]

    return body


def solution(mesh):
    return jax.shard_map(
        make_body(mesh),
        mesh=mesh,
        in_specs=(
            P(("groups", "dp"), "ctx", None),
            P(("dp", "ctx"), None),
            P(("groups", "dp"), "ctx", None),
            P(("groups", "dp"), "ctx", None),
            P(("groups", "dp"), None, "ctx"),
            P(("groups", "dp"), None, "ctx"),
            P(("groups", "dp"), "ctx"),
        ),
        out_specs=P(("groups", "dp"), "ctx", None),
        check_vma=False,
    )
```

```python
import functools

import jax
import jax.numpy as jnp
from jax import lax
from jax.experimental import pallas as pl
from jax.experimental.pallas import tpu as pltpu
from jax.sharding import PartitionSpec as P


very_low = -1e30
AXES = ("groups", "dp", "ctx")
CORES = 2
EXTRA = 16
f32 = jnp.float32
bf16 = jnp.bfloat16


def moves(mesh, where):
    ng, nd, nz = (mesh.shape[a] for a in AXES)
    pairs = []
    for g in range(ng):
        for x in range(nd // CORES):
            for k in range(CORES):
                for z in range(nz):
                    to = where(g, x, k, z)
                    if to is not None:
                        g2, x2, k2, z2 = to
                        source = (g * nd + x * CORES + k) * nz + z
                        pairs.append((source, (g2 * nd + x2 * CORES + k2) * nz + z2))
    return pairs


def lane_scan(values):
    length = values.shape[1]
    lane = lax.broadcasted_iota(jnp.int32, values.shape, 1)
    step = 1
    while step < length:
        moved = pltpu.roll(values, step, 1)
        values = values + jnp.where(lane >= step, moved, jnp.zeros_like(values))
        step *= 2
    return values


def log_sigmoid(x):
    return jnp.minimum(x, 0.0) - jnp.log1p(jnp.exp(-jnp.abs(x)))


def padded(values):
    rows = values.shape[0]
    if rows % 8 == 0:
        return values
    fill = jnp.zeros((8 - rows % 8, values.shape[1]), values.dtype)
    return jnp.concatenate([values, fill], axis=0)


def split_rows(value):
    high = value.astype(bf16)
    rest = value - high.astype(f32)
    mid = rest.astype(bf16)
    low = (rest - mid.astype(f32)).astype(bf16)
    return high, mid, low


def store_message(out_ref, base, size, memory, normer, top):
    out_ref[base : base + size, :] = memory.astype(bf16)
    n_parts = split_rows(normer)
    t_parts = split_rows(jnp.broadcast_to(top, normer.shape))
    row = lax.broadcasted_iota(jnp.int32, (EXTRA, normer.shape[1]), 0)
    block = jnp.zeros((EXTRA, normer.shape[1]), f32)
    for i, part in enumerate(n_parts + t_parts):
        block = jnp.where(row == i, part.astype(f32), block)
    out_ref[base + size : base + size + EXTRA, :] = block.astype(bf16)


def load_message(ref, base, size):
    extra = ref[base + size : base + size + EXTRA, :].astype(f32)
    normer = extra[0:1] + extra[1:2] + extra[2:3]
    top = extra[3:4, 0:1] + extra[4:5, 0:1] + extra[5:6, 0:1]
    return ref[base : base + size, :], normer, top


def weight_kernel(ng, w_ref, send_ref, *refs):
    own, sems = refs[:ng], refs[ng]
    group = lax.axis_index("groups")
    core = lax.rem(lax.axis_index("dp"), CORES)
    half, width = send_ref.shape[1], own[0].shape[1]
    wanted = [((1 - core) * half, send_ref)]
    for r in range(ng):
        wanted.append((core * half + lax.rem(group + r, ng) * width, own[r]))
    fetch(w_ref, wanted, width, sems)


def token_kernel(nx, x_ref, *refs):
    away, sems = refs[: nx - 1], refs[nx - 1]
    x = lax.div(lax.axis_index("dp"), CORES)
    depth = away[0].shape[1]
    wanted = [(lax.rem(x + rel, nx) * depth, away[rel - 1]) for rel in range(1, nx)]
    fetch(x_ref, wanted, depth, sems)


def fetch(ref, wanted, step, sems):
    copies = []
    for i, (column, target) in enumerate(wanted):
        source = ref.at[:, pl.ds(pl.multiple_of(column, step), target.shape[1])]
        copies.append(pltpu.make_async_copy(source, target, sems.at[i]))
        copies[-1].start()
    for each in copies:
        each.wait()


def pack_kernel(own_ref, swapped_ref, out_ref):
    _, width = own_ref.shape
    column = pl.multiple_of(lax.axis_index("groups") * width, width)
    out_ref[0] = own_ref[...]
    out_ref[1] = swapped_ref[:, pl.ds(column, width)]


def state_kernel(heads, ng, *refs):
    k_ref, v_ref, x_ref, gate_ref, forget_ref, reset_ref, xown_ref = refs[:7]
    chunks, sem = refs[7 : 7 + 3 * ng], refs[7 + 3 * ng]
    length = k_ref.shape[0]
    size, vsize = k_ref.shape[1] // heads, v_ref.shape[1] // heads
    group, dp = lax.axis_index("groups"), lax.axis_index("dp")
    depth = xown_ref.shape[1]
    column = pl.multiple_of(lax.div(dp, CORES) * depth, depth)
    copy = pltpu.make_async_copy(x_ref.at[:, pl.ds(column, depth)], xown_ref, sem)
    copy.start()
    count = lane_scan(padded(reset_ref[...].astype(f32)))[0:1]
    cumulative = lane_scan(padded(log_sigmoid(forget_ref[...])))[0:heads]
    total = cumulative[:, length - 1 : length]
    final = count[:, length - 1 : length]
    expo = jnp.where(count == final, total - cumulative + gate_ref[...], very_low)
    top = jnp.max(expo, axis=1, keepdims=True)
    weight = padded(jnp.exp(expo - top)).T
    gap = jnp.where(final > 0, very_low, total)
    for r in range(ng):
        own_ref, msg_ref, side_ref = chunks[3 * r : 3 * r + 3]
        for j in range(heads // ng):
            within = lax.rem(group + r, ng)
            head = j * ng + within

            def pick(values):
                chosen = values[j * ng]
                for i in range(1, ng):
                    chosen = jnp.where(within == i, values[j * ng + i], chosen)
                return chosen

            keys = k_ref[:, pl.ds(pl.multiple_of(head * size, size), size)].astype(f32)
            values = v_ref[:, pl.ds(pl.multiple_of(head * vsize, vsize), vsize)]
            scale = pick([weight[:, h : h + 1] for h in range(heads)])
            this_top = pick([top[h : h + 1] for h in range(heads)])
            this_gap = pick([gap[h : h + 1] for h in range(heads)])
            weighted = (keys * scale).astype(bf16)
            memory = lax.dot_general(
                weighted, values, (((0,), (0,)), ((), ())), preferred_element_type=f32
            )
            normer = jnp.sum(weighted.astype(f32), axis=0, keepdims=True)
            own_ref[j * size : (j + 1) * size, :] = memory
            side_ref[j * 8 : j * 8 + 1, :] = normer
            side_ref[j * 8 + 1 : j * 8 + 2, :] = jnp.broadcast_to(this_top, normer.shape)
            side_ref[j * 8 + 2 : j * 8 + 3, :] = jnp.broadcast_to(this_gap, normer.shape)
            store_message(msg_ref, j * (size + EXTRA), size, memory, normer, this_top)
    copy.wait()


def join(slots, prev_ref, own_ref, side_ref, out_ref):
    size = own_ref.shape[0] // slots
    stride = size + EXTRA
    for h in range(slots):
        memory, normer, top = load_message(prev_ref, h * stride, size)
        own_normer = side_ref[h * 8 : h * 8 + 1, :]
        own_top = side_ref[h * 8 + 1 : h * 8 + 2, 0:1]
        gap = side_ref[h * 8 + 2 : h * 8 + 3, 0:1]
        shifted = top + gap
        both = jnp.maximum(shifted, own_top)
        early = jnp.exp(shifted - both)
        late = jnp.exp(own_top - both)
        joined = early * memory.astype(f32) + late * own_ref[h * size : (h + 1) * size, :]
        normers = early * normer + late * own_normer
        store_message(out_ref, h * stride, size, joined, normers, both)


def combine_kernel(slots, sender, prev_ref, own_ref, side_ref, out_ref):
    place = lax.axis_index("ctx")

    @pl.when(place == sender)
    def _():
        join(slots, prev_ref, own_ref, side_ref, out_ref)

    @pl.when(place != sender)
    def _():
        out_ref[...] = prev_ref[...]


def mix_kernel(message_ref, piece_ref, out_ref):
    place = lax.axis_index("ctx")
    rows = piece_ref.shape[1]

    @pl.when(place == 0)
    def _():
        out_ref[...] = message_ref[...]

    @pl.when(place != 0)
    def _():
        for j in range(CORES):
            out_ref[j * rows : (j + 1) * rows, :] = piece_ref[j]
        rest = out_ref.shape[0] - CORES * rows
        out_ref[CORES * rows :, :] = jnp.zeros((rest, out_ref.shape[1]), out_ref.dtype)


def pick_kernel(inner_ref, outer_ref, out_ref):
    place = lax.axis_index("ctx")
    rows = out_ref.shape[1]
    inner = jnp.logical_or(place == 1, place == 2)

    @pl.when(inner)
    def _():
        out_ref[...] = inner_ref[...]

    @pl.when(jnp.logical_not(inner))
    def _():
        for j in range(CORES):
            out_ref[j] = outer_ref[j * rows : (j + 1) * rows, :]


def away_kernel(nz, ng, phase, swapped, count, *refs):
    first = 2 if phase else 1
    tokens, parts = refs[:count], refs[count : count + first + nz - 1]
    outs, whole = refs[count + len(parts) : -1], refs[-1]
    rows, width = parts[-1].shape[1:]
    place, group = lax.axis_index("ctx"), lax.axis_index("groups")
    core = lax.rem(lax.axis_index("dp"), CORES)
    if phase:
        column = pl.multiple_of(lax.rem(group + phase, ng) * width, width)
        values = [(parts[0][...], parts[1][:, pl.ds(column, width)])]
    else:
        values = [(parts[0][0], parts[0][1])]
    for part in parts[first:]:
        values.append((part[0], part[1]))
    for s in range(nz):
        source = place ^ s
        if swapped and s >= 2:
            inner = jnp.logical_or(place == 1, place == 2)
            source = jnp.where(inner, place ^ (5 - s), source)
        for j in range(CORES):
            owner = lax.rem(core + j, CORES)
            row = pl.multiple_of((owner * nz + source) * rows, rows)
            whole[pl.ds(row, rows), :] = values[s][j]
    for token, out in zip(tokens, outs):
        value = jnp.dot(token[...], whole[...], preferred_element_type=f32)
        out[...] = value.astype(out.dtype)


def keep_kernel(*refs):
    tokens, whole, outs = refs[:CORES], refs[CORES], refs[CORES + 1 :]
    for token, out in zip(tokens, outs):
        out[...] = jnp.dot(token[...], whole[...], preferred_element_type=f32)


def head_of(j, r, ng):
    slot = lax.rem(lax.rem(lax.axis_index("dp"), CORES) + j, CORES)
    return slot * ng + lax.rem(lax.axis_index("groups") + r, ng)


def decay_kernel(ng, gate_ref, forget_ref, reset_ref, *outs):
    length = reset_ref.shape[1]
    t_at = lax.broadcasted_iota(jnp.int32, (length, length), 0)
    s_at = lax.broadcasted_iota(jnp.int32, (length, length), 1)
    pairs = [(j, r) for r in range(ng) for j in range(CORES)]
    forget = [log_sigmoid(forget_ref[pl.ds(head_of(j, r, ng), 1), :]) for j, r in pairs]
    running = lane_scan(padded(jnp.concatenate([reset_ref[...].astype(f32)] + forget, axis=0)))
    running_rows = running.T
    count, count_rows = running[0:1], running_rows[:, 0:1]
    linked = jnp.logical_and(count_rows == count, t_at >= s_at)
    for at, (j, r) in enumerate(pairs):
        decay_ref, column_ref = outs[2 * r], outs[2 * r + 1]
        cum_t = running_rows[:, 1 + at : 2 + at]
        exponent = jnp.where(
            linked,
            cum_t - running[1 + at : 2 + at] + gate_ref[pl.ds(head_of(j, r, ng), 1), :],
            very_low,
        )
        top = jnp.max(exponent, axis=1, keepdims=True)
        decay_ref[j] = jnp.exp(exponent - top)
        lane = lax.broadcasted_iota(jnp.int32, (length, 128), 1)
        columns = jnp.where(lane == 0, top, jnp.where(lane == 1, cum_t, count_rows))
        column_ref[j] = columns


def read_kernel(heads, ng, nx, hops, phase, *refs):
    partials = [refs[j * nx : (j + 1) * nx] for j in range(CORES)]
    k_ref, v_ref, decay_ref, column_ref = refs[CORES * nx : CORES * nx + 4]
    at = CORES * nx + 4
    states = refs[at : at + hops]
    out_ref, state, result, sem, out_sems = refs[at + hops + (1 if phase else 0) :]
    size, vsize = k_ref.shape[1] // heads, v_ref.shape[1] // heads
    factor = size ** (-0.5)
    stride = size + EXTRA
    place = lax.axis_index("ctx")
    core = lax.rem(lax.axis_index("dp"), CORES)
    for h in range(hops):

        @pl.when(place == h + 1)
        def _():
            pltpu.make_async_copy(states[h], state, sem).start()

    @pl.when(place == 0)
    def _():
        state[...] = jnp.zeros_like(state)

    queries, scores = [], []
    for j in range(CORES):
        head = head_of(j, phase, ng)
        total = partials[j][0][...]
        for other in partials[j][1:]:
            total = total + other[...].astype(f32)
        query = total.astype(bf16)
        keys = k_ref[:, pl.ds(pl.multiple_of(head * size, size), size)]
        queries.append(query)
        scores.append(
            lax.dot_general(query, keys, (((1,), (1,)), ((), ())), preferred_element_type=f32)
        )

    @pl.when(place > 0)
    def _():
        pltpu.make_async_copy(states[0], state, sem).wait()

    copies = []
    for j in range(CORES):
        head = head_of(j, phase, ng)
        query = queries[j]
        column = pl.multiple_of(head * vsize, vsize)
        values = v_ref[:, pl.ds(column, vsize)]
        base = pl.multiple_of(lax.rem(core + j, CORES) * stride, EXTRA)
        memory = state[pl.ds(base, size), :]
        extra = state[pl.ds(pl.multiple_of(base + size, EXTRA), EXTRA), :].astype(f32)
        normer = (extra[0:1] + extra[1:2] + extra[2:3]).astype(bf16).astype(f32)
        top = extra[3:4, 0:1] + extra[4:5, 0:1] + extra[5:6, 0:1]
        top = jnp.where(place == 0, very_low, top)
        columns = column_ref[j]
        block_max, cum_t, count_rows = columns[:, 0:1], columns[:, 1:2], columns[:, 2:3]
        carried = jnp.where(count_rows == 0.0, cum_t + top, very_low)
        row_max = jnp.maximum(block_max, carried)
        weighted = (decay_ref[j] * (scores[j] * factor)).astype(bf16)
        within = jnp.exp(block_max - row_max)
        scale = jnp.exp(carried - row_max) * factor
        cross = jnp.dot(query, memory, preferred_element_type=f32)
        inter = jnp.sum(query.astype(f32) * normer, axis=1, keepdims=True)
        numerator = (
            within * jnp.dot(weighted, values, preferred_element_type=f32) + scale * cross
        )
        denominator = (
            within * jnp.sum(weighted.astype(f32), axis=1, keepdims=True) + scale * inter
        )
        floor = jnp.exp(jnp.maximum(-row_max, 0.0))
        result[j] = (numerator / jnp.maximum(jnp.abs(denominator), floor)).astype(bf16)
        copy = pltpu.make_async_copy(
            result.at[j], out_ref.at[:, pl.ds(column, vsize)], out_sems.at[j]
        )
        copy.start()
        copies.append(copy)
    for copy in copies:
        copy.wait()


VMEM = pl.BlockSpec(memory_space=pltpu.VMEM)
ANY = pl.BlockSpec(memory_space=pl.ANY)


def links(z):
    return {z: z + 1, z + 1: z}


def compact(mesh):
    return mesh.shape["ctx"] == 4 and mesh.shape["groups"] == CORES == 2


def make_body(mesh):
    ng, nd, nz = (mesh.shape[a] for a in AXES)
    nx = nd // CORES

    def send(value, where):
        return lax.ppermute(value, AXES, moves(mesh, where))

    def over_core(value):
        return send(value, lambda g, x, k, z: (g, x, 1 - k, z))

    def call(kernel, *args, **options):
        params = pltpu.CompilerParams(vmem_limit_bytes=20 * 2**20)
        return pl.pallas_call(kernel, compiler_params=params, **options)(*args)

    def body(normed_input, query_weight, key_vectors, value_vectors, input_gate, forget_gate, resets):
        _, length, features = normed_input.shape
        heads = input_gate.shape[1]
        columns = query_weight.shape[1]
        width = columns // (ng * CORES)
        size = columns // heads
        keys, values = key_vectors[0], value_vectors[0]
        gate, forget = input_gate[0], forget_gate[0]
        vwidth = values.shape[1]
        half = columns // CORES
        depth = features // nx
        flat = normed_input[0]

        stride = size + EXTRA
        vsize = vwidth // heads
        slots = heads // ng
        message = jax.ShapeDtypeStruct((slots * stride, vsize), bf16)
        block = jax.ShapeDtypeStruct((length, depth), flat.dtype)
        hbm_tokens = pltpu.with_memory_space_constraint(flat, pltpu.HBM)
        hbm_weight = pltpu.with_memory_space_constraint(query_weight, pltpu.HBM)
        rows = query_weight.shape[0]
        quarter = jax.ShapeDtypeStruct((rows, width), query_weight.dtype)
        sliced = call(
            functools.partial(weight_kernel, ng),
            hbm_weight,
            out_shape=(
                jax.ShapeDtypeStruct((rows, half), query_weight.dtype),
                *[quarter] * ng,
            ),
            in_specs=[ANY],
            out_specs=(VMEM,) * (1 + ng),
            scratch_shapes=[pltpu.SemaphoreType.DMA((1 + ng,))],
        )
        leaving = call(
            functools.partial(token_kernel, nx),
            hbm_tokens,
            out_shape=(block,) * (nx - 1),
            in_specs=[ANY],
            out_specs=(VMEM,) * (nx - 1),
            scratch_shapes=[pltpu.SemaphoreType.DMA((nx - 1,))],
        )
        swapped = over_core(sliced[0])
        own_parts = sliced[1 : 1 + ng]
        arrived = [
            send(leaving[rel - 1], lambda g, x, k, z: (g, (x + rel) % nx, k, z))
            for rel in range(1, nx)
        ]
        packed = call(
            pack_kernel,
            own_parts[0], swapped,
            out_shape=jax.ShapeDtypeStruct((CORES, rows, width), bf16),
            in_specs=[VMEM] * 2,
            out_specs=VMEM,
        )
        prepared = call(
            functools.partial(state_kernel, heads, ng),
            keys, values, hbm_tokens, gate, forget, resets,
            out_shape=(
                block,
                *[
                    jax.ShapeDtypeStruct((slots * size, vsize), f32),
                    message,
                    jax.ShapeDtypeStruct((slots * 8, vsize), f32),
                ]
                * ng,
            ),
            in_specs=[VMEM] * 2 + [ANY] + [VMEM] * 3,
            out_specs=(VMEM,) * (1 + 3 * ng),
            scratch_shapes=[pltpu.SemaphoreType.DMA(())],
        )
        tokens = [prepared[0]]
        tokens.append(over_core(tokens[0]))
        for rel, value in enumerate(arrived):
            tokens.extend([value, over_core(value)])
        pieces = [[packed]] + [[own_parts[r], swapped] for r in range(1, ng)]

        def over_ctx(value, targets):
            return send(
                value,
                lambda g, x, k, z: (g, x, k, targets[z]) if z in targets else (g, x, 1 - k, z),
            )

        own = [prepared[1 + 3 * r] for r in range(ng)]
        first = [prepared[2 + 3 * r] for r in range(ng)]
        side = [prepared[3 + 3 * r] for r in range(ng)]
        states = [[] for _ in range(ng)]

        def extend(hop, r):
            message_out = call(
                functools.partial(combine_kernel, slots, hop - 1),
                states[r][-1], own[r], side[r],
                out_shape=message,
                in_specs=[VMEM] * 3,
                out_specs=VMEM,
            )
            states[r].append(over_ctx(message_out, links(hop - 1)))

        if compact(mesh):
            near = over_ctx(packed, {z: z ^ 1 for z in range(nz)})
            middle = over_ctx(packed, links(1))
            across = over_ctx(near, links(1))
            gathered = {1: near}
            for r, inside in enumerate((middle, across)):
                mixed = call(
                    mix_kernel,
                    first[r], inside,
                    out_shape=message,
                    in_specs=[VMEM] * 2,
                    out_specs=VMEM,
                )
                outside = over_ctx(mixed, {**links(0), **links(2)})
                states[r].append(outside)
                gathered[r + 2] = call(
                    pick_kernel,
                    inside, outside,
                    out_shape=jax.ShapeDtypeStruct(packed.shape, bf16),
                    in_specs=[VMEM] * 2,
                    out_specs=VMEM,
                )
        else:
            gathered = {s: over_ctx(packed, {z: z ^ s for z in range(nz)}) for s in range(1, nz)}
            for r in range(ng):
                states[r].append(over_ctx(first[r], links(0)))
        for hop in range(2, nz):
            for r in range(ng):
                extend(hop, r)
        for s in range(1, nz):
            pieces[0].append(gathered[s])
            for r in range(1, ng):
                pieces[r].append(send(gathered[s], lambda g, x, k, z: ((g - r) % ng, x, k, z)))
        decays = call(
            functools.partial(decay_kernel, ng),
            gate, forget, resets,
            out_shape=(
                jax.ShapeDtypeStruct((CORES, length, length), f32),
                jax.ShapeDtypeStruct((CORES, length, 128), f32),
            )
            * ng,
            in_specs=[VMEM] * 3,
            out_specs=(VMEM,) * (2 * ng),
        )
        hidden = None
        for r in range(ng):
            piece = jax.ShapeDtypeStruct((length, width), f32)
            small = jax.ShapeDtypeStruct((length, width), bf16)
            count = CORES * (nx - 1)
            sent = call(
                functools.partial(away_kernel, nz, ng, r, compact(mesh), count),
                *tokens[CORES:], *pieces[r],
                out_shape=(small,) * count + (jax.ShapeDtypeStruct((depth, width), bf16),),
                in_specs=[VMEM] * (count + len(pieces[r])),
                out_specs=(VMEM,) * (count + 1),
            )
            kept = call(
                keep_kernel,
                *tokens[:CORES], sent[-1],
                out_shape=(piece,) * CORES,
                in_specs=[VMEM] * (CORES + 1),
                out_specs=(VMEM,) * CORES,
            )
            sums = [*kept, *sent[:-1]]
            partials = [[sums[0]], [over_core(sums[1])]]
            for rel in range(1, nx):
                for j in range(CORES):
                    partials[j].append(
                        send(
                            sums[CORES * rel + j], lambda g, x, k, z: (g, (x - rel) % nx, k ^ j, z)
                        )
                    )
            count = CORES * nx + 4 + nz - 1
            hidden = call(
                functools.partial(read_kernel, heads, ng, nx, nz - 1, r),
                *partials[0], *partials[1], keys, values, *decays[2 * r : 2 * r + 2],
                *states[r], *([hidden] if r else []),
                out_shape=jax.ShapeDtypeStruct((length, vwidth), bf16),
                in_specs=[VMEM] * (CORES * nx + 4) + [ANY] * (nz - 1 + (1 if r else 0)),
                out_specs=ANY,
                input_output_aliases={count: 0} if r else {},
                scratch_shapes=[
                    pltpu.VMEM(message.shape, bf16),
                    pltpu.VMEM((CORES, length, vsize), bf16),
                    pltpu.SemaphoreType.DMA(()),
                    pltpu.SemaphoreType.DMA((CORES,)),
                ],
            )
        return hidden[None]

    return body


def solution(mesh):
    return jax.shard_map(
        make_body(mesh),
        mesh=mesh,
        in_specs=(
            P(("groups", "dp"), "ctx", None),
            P(("dp", "ctx"), None),
            P(("groups", "dp"), "ctx", None),
            P(("groups", "dp"), "ctx", None),
            P(("groups", "dp"), None, "ctx"),
            P(("groups", "dp"), None, "ctx"),
            P(("groups", "dp"), "ctx"),
        ),
        out_specs=P(("groups", "dp"), "ctx", None),
        check_vma=False,
    )
```
